32 devices in a mesh: beam: 2 (over y), fft: 4 (over z), chan: 4 (over x, core).
Axes of the slice: x: 2, y: 2, z: 4, core: 2. Of those that a mesh axis runs over, the one named last changes fastest.
Arguments:
- filterbank: bfloat16 [8192, 16384], P(('beam', 'chan'), 'fft'), parts along dimension 0, may hold values from -6 to 6
- delays: int32 [4096, 16], P('chan'), may hold values from 0 to 15, as said below
- template_bank: bfloat16 [2, 128, 32], replicated, may hold values from -1 to 1
- accel_index: int32 [64], replicated, may hold values from 0 to 127, as said below
Outputs:
- peaks: float32 [32, 64, 64], P(('beam', 'fft', 'chan')), parts along dimension 0
- energy: float32 [32], P(('beam', 'fft', 'chan')), parts along dimension 0
The draws below stay inside these ranges and needn't reach their ends.
There are 2 independent parts, one for each index of `beam`. The reference program is written for one: setup_inputs(seed, part) draws one part's arguments, and reference() takes and returns one part's arrays. A program takes and returns all parts, laid end to end along the dimension named above; an argument that names none is the same for every part. Nothing has to cross between parts.
Inputs may be any that keep to these rules, and one draw needn't show every extreme that they name: `delays`: follows the cold-plasma law: proportional to the trial measure times the channel's inverse squared frequency less that of the band's top, rounded down; the trial measures rise over the whole range; non-increasing along channels and non-decreasing along trial measures; the first channel reaches 15 at the last trial measure. `accel_index`: distinct and increasing; the first is 0 and the last is 127.
All inputs are finite; a program needn't handle non-finite values.
Results may differ from the reference program's by a relative error of at most 0.0021.
Values may be sent and summed in bfloat16 or wider, within the bound.
A program may use at most 64 MiB of HBM per device.

```python
import jax
import jax.numpy as jnp
from jax import lax

CHAN = 4096
MAXD = 16
WID = 32
NACC = 64
ZBANK = 128
NDM = 16
NSAMP = 16384


def draw_accel_index(key, part):
    interior = jax.random.permutation(jax.random.fold_in(key, 11), ZBANK - 2)[:NACC - 2] + 1
    chosen = jnp.concatenate([jnp.zeros((1,), jnp.int32), interior.astype(jnp.int32), jnp.full((1,), ZBANK - 1, jnp.int32)])
    return jnp.sort(chosen)


def draw_delays(key, part):
    steps_drawn = jax.random.randint(jax.random.fold_in(key, 23), (NDM,), 1, 3).astype(jnp.int32)
    rising = jnp.cumsum(steps_drawn).astype(jnp.int32) - steps_drawn[0]
    last_step = rising[NDM - 1]
    freqs = CHAN + jnp.arange(CHAN, dtype=jnp.int32)
    top_freq = 2 * CHAN
    scale_top = 2 ** 30 // (top_freq * top_freq)
    lags = 2 ** 30 // (freqs * freqs) - scale_top
    lags = lags.astype(jnp.int32)
    lowest = lags[0]
    numer = lags[:, None] * (MAXD - 1) * rising[None, :]
    table = numer // (lowest * last_step)
    return table.astype(jnp.int32)


def steps_of(rng, shape, cuts, low, top_value):
    def one(position, blocks):
        draws = jax.random.uniform(jax.random.fold_in(jax.random.fold_in(rng, 6), position), (blocks,), jnp.float32, low / len(cuts), top_value / len(cuts))
        return jnp.repeat(jnp.exp(draws), shape[position] // blocks).reshape((-1,) + (1,) * (len(shape) - position - 1))

    gain = one(*cuts[0])
    for cut in cuts[1:]:
        gain = gain * one(*cut)
    return gain


def gaussian(own_key, shape, scale, most, split=(), held_as=jnp.bfloat16):
    gain = steps_of(own_key, shape, split, -0.22, 0.18) if split else 1.0
    result = jax.random.normal(own_key, shape, jnp.float32) * scale * gain
    return jnp.minimum(jnp.maximum(result, -most), most).astype(held_as)


def setup_inputs(seed: int = 0, part: int = 0) -> dict:
    key_list = jax.random.split(jax.random.key(seed), 5)
    part_keys = jax.random.split(jax.random.fold_in(key_list[4], part), 5)
    filterbank = gaussian(part_keys[0], (CHAN, NSAMP), 1.0, 6.0, ((0, 4), (1, 4)))
    delays = draw_delays(jax.random.fold_in(key_list[4], 71), part)
    template_bank = gaussian(key_list[2], (2, ZBANK, WID), WID ** -0.5, 1.0)
    accel_index = draw_accel_index(jax.random.fold_in(key_list[4], 71), part)
    return {"filterbank": filterbank, "delays": delays, "template_bank": template_bank, "accel_index": accel_index}


def reference(filterbank, delays, template_bank, accel_index):
    channels, length = filterbank.shape
    block_count = length // 128
    padded = jnp.concatenate([filterbank, jnp.zeros((channels, MAXD * 128), filterbank.dtype)], axis=1)
    padded = padded.reshape(channels, block_count + MAXD, 128)
    starts = jnp.arange(block_count, dtype=jnp.int32)

    def one_measure(column):
        index_table = starts[None, :] + column.astype(jnp.int32)[:, None]
        picked = jnp.take_along_axis(padded, index_table[:, :, None], axis=1)
        return jnp.sum(picked.astype(jnp.float32), axis=0).reshape(length)

    series = lax.map(one_measure, delays.T) * (CHAN ** -0.5)
    bin_total = length // 2
    transform = jnp.fft.fft(series, axis=1)[:, :bin_total] * (length ** -0.5)
    spec_real = jnp.real(transform).astype(jnp.float32)
    spec_imag = jnp.imag(transform).astype(jnp.float32)
    round_real = spec_real.astype(jnp.bfloat16)
    round_imag = spec_imag.astype(jnp.bfloat16)
    kernel_stack = jnp.concatenate([template_bank[0][accel_index], template_bank[1][accel_index]], axis=0)
    templates = accel_index.shape[0]
    lead_taps = WID // 2

    def one_row(pair):
        row_real, row_imag = pair
        pad_real = jnp.pad(row_real, (lead_taps, WID - lead_taps))
        pad_imag = jnp.pad(row_imag, (lead_taps, WID - lead_taps))
        win_real = jnp.stack([pad_real[lag_index:lag_index + bin_total] for lag_index in range(WID)], axis=0)
        win_imag = jnp.stack([pad_imag[lag_index:lag_index + bin_total] for lag_index in range(WID)], axis=0)
        from_real = jnp.dot(kernel_stack, win_real, preferred_element_type=jnp.float32)
        from_imag = jnp.dot(kernel_stack, win_imag, preferred_element_type=jnp.float32)
        out_real = from_real[:templates] - from_imag[templates:]
        out_imag = from_imag[:templates] + from_real[templates:]
        power = out_real * out_real + out_imag * out_imag
        return jnp.max(power.reshape(templates, bin_total // 128, 128), axis=2)

    peaks = lax.map(one_row, (round_real, round_imag))
    energy = jnp.sum(spec_real * spec_real + spec_imag * spec_imag, axis=1)
    return (peaks, energy)
```

```python
import functools

import jax
import jax.numpy as jnp
import ml_dtypes
import numpy as np
from jax import lax
from jax.experimental import pallas as pl
from jax.experimental.pallas import tpu as pltpu
from jax.sharding import PartitionSpec as P

MAXD = 16
LANES = 128
CHUNKS = 4
MESH = pl.DeviceIdType.MESH


def halves(table):
    high = table.astype(np.float32).astype(ml_dtypes.bfloat16)
    low = (table - high.astype(np.float64)).astype(np.float32).astype(ml_dtypes.bfloat16)
    return high, low


def tables(length, channels_total):
    wide = length // LANES
    half = wide // 2
    rows = np.arange(LANES)
    cols = np.arange(wide)
    outs = np.arange(half)
    first = 2 * np.pi * (rows[:, None] * rows[None, :] % LANES) / LANES
    one = np.concatenate([np.cos(first), -np.sin(first)], axis=0)
    turn = 2 * np.pi * (rows[:, None] * cols[None, :] % length) / length
    scale = channels_total ** -0.5 * length ** -0.5
    twist = np.stack([np.cos(turn), np.sin(turn)]) * scale
    second = 2 * np.pi * (cols[:, None] * outs[None, :] % wide) / wide
    c2, s2 = np.cos(second), np.sin(second)
    real = np.concatenate([c2, s2], axis=0)
    imag = np.concatenate([-s2, c2], axis=0)
    two = np.concatenate([real, real, imag, imag], axis=1)
    one = np.concatenate(halves(one), axis=1)
    two = np.stack(halves(two))
    return jnp.asarray(one), jnp.asarray(twist, jnp.float32), jnp.asarray(two)


def split(x):
    high = x.astype(jnp.bfloat16)
    return high, (x - high.astype(jnp.float32)).astype(jnp.bfloat16)


def dot(a, b):
    return jnp.dot(a, b, preferred_element_type=jnp.float32)


def kernel(
    sizes,
    fb_ref, delay_hbm, bank_hbm, accel_hbm, one_hbm, twist_hbm, two_hbm,
    peaks_ref, energy_ref,
    delay_ref, xbuf, picked, acc, early, late, early_in, late_in, grid_ref,
    bank_ref, accel_ref, one_ref, twist_ref, two_ref, tmat,
    lsem, fsem, tsem, early_out_sem, early_in_sem, late_out_sem, late_in_sem,
):
    fft, xs, cores, dms, blocks = sizes
    chan = xs * cores
    cut = blocks // 2 + MAXD
    f = lax.axis_index("fft")
    c = lax.axis_index("chan")
    x, core = c // cores, c % cores
    columns = fb_ref.shape[1]
    chunk = columns // CHUNKS
    count = fft * chan
    partners = [
        (g, s, k) for g in range(fft) for s in range(xs) for k in range(cores) if (g, s, k) != (0, 0, 0)
    ]
    far_first = sorted(partners, key=lambda p: (-min(p[0], fft - p[0]) - p[1], -p[2]))

    def fetch(i):
        return pltpu.make_async_copy(
            fb_ref.at[:, i * chunk:(i + 1) * chunk], xbuf.at[i], fsem.at[i]
        )

    loads = [
        pltpu.make_async_copy(a, b, tsem.at[i])
        for i, (a, b) in enumerate(
            [
                (bank_hbm, bank_ref), (accel_hbm, accel_ref), (one_hbm, one_ref),
                (twist_hbm, twist_ref), (two_hbm, two_ref),
            ]
        )
    ]
    lags = pltpu.make_async_copy(delay_hbm, delay_ref, lsem)
    lags.start()
    order = list(range(CHUNKS))[::-1]
    for n, i in enumerate(order):
        fetch(i).start(priority=min(n, 1))

    def place(p):
        g, s, k = p
        return (f + g) % fft, ((x + s) % xs) * cores + (core + k) % cores

    barrier = pltpu.get_barrier_semaphore()
    for p in partners:
        g, d = place(p)
        pl.semaphore_signal(barrier, inc=1, device_id={"fft": g, "chan": d}, device_id_type=MESH)

    acc[...] = jnp.zeros_like(acc)
    lags.wait()
    lag = delay_ref[...]
    for o in range(MAXD):
        picked[(MAXD - 1 - o) * dms:(MAXD - o) * dms, :] = jnp.where(lag == o, 1.0, 0.0).astype(
            jnp.bfloat16
        )

    def slot(p):
        return (p[0] * xs + p[1]) * cores + p[2]

    def send(p, out, into, out_sem, in_sem):
        g, d = place(p)
        return pltpu.make_async_remote_copy(
            out.at[g * chan + d], into.at[slot(p)], out_sem, in_sem,
            device_id={"fft": g, "chan": d}, device_id_type=MESH,
        )

    def send_early(p):
        return send(p, early, early_in, early_out_sem, early_in_sem)

    def send_late(p):
        return send(p, late, late_in, late_out_sem, late_in_sem)

    def everything(ref, sem):
        part = ref.at[pl.ds(1, count - 1)]
        return pltpu.make_async_copy(part, part, sem)

    for n, i in enumerate(order):
        fetch(i).wait()
        for b in range(chunk // 256):
            y = dot(picked[...], xbuf[i, :, b * 256:(b + 1) * 256])
            for h in range(2):
                row = (i * (chunk // LANES) + 2 * b + h + 1) * dms
                acc[row:row + MAXD * dms, :] += y[:, h * LANES:(h + 1) * LANES]
        if n == CHUNKS // 2 - 1:
            for d in range(count):
                early[d] = acc[pl.ds(cut * dms + d, blocks + MAXD - cut, stride=dms), :].astype(
                    jnp.bfloat16
                )
            pl.semaphore_wait(barrier, len(partners))
            for p in far_first:
                send_early(p).start()
    for d in range(count):
        late[d] = acc[pl.ds(d, cut, stride=dms), :].astype(jnp.bfloat16)
    for p in far_first:
        send_late(p).start()
    for load in loads:
        load.start()

    loads[0].wait()
    loads[1].wait()
    accel = accel_ref[...]
    bank = bank_ref.shape[2]
    accels = accel.shape[1]
    taps = bank_ref.shape[1]
    chosen = jnp.where(
        lax.broadcasted_iota(jnp.int32, (bank, accels), 0) == accel, 1.0, 0.0
    ).astype(jnp.bfloat16)
    rows = []
    for part_index in range(2):
        row = dot(bank_ref[part_index], chosen)
        row = jnp.concatenate([row, jnp.zeros((LANES - taps, accels), jnp.float32)], axis=0)
        rows.append(row.T)
    for kk in range(LANES // 2):
        for part_index in range(2):
            shifted = pltpu.roll(rows[part_index], kk, 1) if kk else rows[part_index]
            tmat[kk * accels:(kk + 1) * accels, part_index * LANES:(part_index + 1) * LANES] = (
                shifted.astype(jnp.bfloat16)
            )
    for load in loads[2:]:
        load.wait()

    own = f * chan + c
    everything(early_in, early_in_sem).wait()
    everything(late_in, late_in_sem).wait()

    def gathered(z, own_ref, in_ref, lo, hi):
        base = ((f + fft - z) % fft) * chan
        total = None
        for k in range(chan):
            value = in_ref[base + k, lo:hi, :].astype(jnp.float32)
            total = value if total is None else total + value
        return total

    early_in[0] = early[own]
    late_in[0] = late[own]
    for z in range(fft):
        body = gathered(z, late, late_in, MAXD, cut)
        if z + 1 < fft:
            tail = gathered(z, early, early_in, 0, blocks + MAXD - cut)
            lead = gathered(z + 1, late, late_in, 0, MAXD)
            gap = tail.shape[0] - MAXD
            if gap:
                tail = jnp.concatenate([tail[:gap], tail[gap:] + lead], axis=0)
            else:
                tail = tail + lead
        else:
            tail = gathered(z, early, early_in, 0, blocks + MAXD - cut)
        grid_ref[z * blocks:z * blocks + cut - MAXD, :] = body
        grid_ref[z * blocks + cut - MAXD:(z + 1) * blocks, :] = tail

    wide = grid_ref.shape[0]
    half = wide // 2
    data = grid_ref[...] if wide == LANES else grid_ref[...].reshape(LANES, wide)
    high, low = split(data)
    both = jnp.concatenate(
        [
            jnp.concatenate([high, low], axis=1),
            jnp.concatenate([high, jnp.zeros_like(low)], axis=1),
        ],
        axis=0,
    )
    mixed = dot(one_ref[...], both)
    mixed = mixed[:, :wide] + mixed[:, wide:]
    re, im = mixed[:LANES], mixed[LANES:]
    tc, ts = twist_ref[0], twist_ref[1]
    turned = jnp.concatenate([re * tc + im * ts, im * tc - re * ts], axis=1)
    high, low = split(turned)
    spec = dot(high, two_ref[0]) + dot(low, two_ref[0]) + dot(high, two_ref[1])

    lane = lax.broadcasted_iota(jnp.int32, (16, 2 * half), 1)
    low64 = lax.broadcasted_iota(jnp.int32, (64, 2 * half), 1) < half
    low16 = lane < half
    sides = []
    square = jnp.zeros((LANES, 2 * half), jnp.float32)
    for part_index in range(2):
        o = spec[:, part_index * 2 * half:(part_index + 1) * 2 * half]
        square = square + o * o
        before = jnp.where(lane == 0, 0.0, pltpu.roll(o[LANES - 16:], 1, 1))
        after = jnp.where(lane == 2 * half - 1, 0.0, pltpu.roll(o[:16], 2 * half - 1, 1))
        sides.append(
            jnp.concatenate(
                [
                    jnp.where(low16, before, o[48:64]),
                    jnp.where(low64, o[:64], o[64:]),
                    jnp.where(low16, o[64:80], after),
                    jnp.zeros((32, 2 * half), jnp.float32),
                ],
                axis=0,
            ).astype(jnp.bfloat16)
        )
    energy_ref[0] = jnp.sum(square) * 0.5
    sr, si = sides
    window = jnp.concatenate(
        [jnp.concatenate([sr, si], axis=1), jnp.concatenate([-si, sr], axis=1)], axis=0
    )
    best = jnp.zeros((accels, 2 * half), jnp.float32)
    group = 8
    for g in range(LANES // 2 // group):
        out = dot(tmat[g * group * accels:(g + 1) * group * accels, :], window)
        for kk in range(group):
            rr = out[kk * accels:(kk + 1) * accels, :2 * half]
            ii = out[kk * accels:(kk + 1) * accels, 2 * half:]
            best = jnp.maximum(best, rr * rr + ii * ii)
    best = jnp.maximum(best, pltpu.roll(best, half, 1))
    peaks_ref[0] = best[:, :half]
    everything(early, early_out_sem).wait()
    everything(late, late_out_sem).wait()


def solution(mesh):
    fft, chan = mesh.shape["fft"], mesh.shape["chan"]
    cores = 2
    xs = chan // cores

    def body(filterbank, delays, template_bank, accel_index):
        channels, samples = filterbank.shape
        dms = delays.shape[1]
        accels = accel_index.shape[0]
        length = samples * fft
        blocks = samples // LANES
        wide = length // LANES
        cut = blocks // 2 + MAXD
        rest = blocks + MAXD - cut
        one, twist, two = tables(length, channels * chan)
        bank = template_bank.transpose(0, 2, 1)
        accel = accel_index[None, :]
        f32, bf16 = jnp.float32, jnp.bfloat16
        dma = pltpu.SemaphoreType.DMA
        hbm = pl.BlockSpec(memory_space=pltpu.HBM)
        vmem = pl.BlockSpec(memory_space=pltpu.VMEM)

        def like(a):
            return pltpu.VMEM(a.shape, a.dtype)

        return pl.pallas_call(
            functools.partial(kernel, (fft, xs, cores, dms, blocks)),
            out_shape=(
                jax.ShapeDtypeStruct((1, accels, wide // 2), f32),
                jax.ShapeDtypeStruct((1,), f32),
            ),
            in_specs=[hbm] * 7,
            out_specs=(vmem, pl.BlockSpec(memory_space=pltpu.SMEM)),
            scratch_shapes=[
                pltpu.VMEM((dms, channels), jnp.int32),
                pltpu.VMEM((CHUNKS, channels, samples // CHUNKS), bf16),
                pltpu.VMEM((MAXD * dms, channels), bf16),
                pltpu.VMEM(((blocks + MAXD) * dms, LANES), f32),
                pltpu.VMEM((dms, rest, LANES), bf16),
                pltpu.VMEM((dms, cut, LANES), bf16),
                pltpu.VMEM((dms, rest, LANES), bf16),
                pltpu.VMEM((dms, cut, LANES), bf16),
                pltpu.VMEM((wide, LANES), f32),
                like(bank), like(accel), like(one), like(twist), like(two),
                pltpu.VMEM((LANES // 2 * accels, 2 * LANES), bf16),
                dma, dma((CHUNKS,)), dma((5,)), dma, dma, dma, dma,
            ],
            compiler_params=pltpu.CompilerParams(
                collective_id=0, has_side_effects=True, vmem_limit_bytes=56 * 2 ** 20
            ),
            name="search",
        )(filterbank, delays.T, bank, accel, one, twist, two)

    in_specs = (P(("beam", "chan"), "fft"), P("chan", None), P(), P())
    out_specs = (P(("beam", "fft", "chan"), None, None), P(("beam", "fft", "chan")))
    return jax.shard_map(body, mesh=mesh, in_specs=in_specs, out_specs=out_specs, check_vma=False)
```

```python
import functools

import jax
import jax.numpy as jnp
import ml_dtypes
import numpy as np
from jax import lax
from jax.experimental import pallas as pl
from jax.experimental.pallas import tpu as pltpu
from jax.sharding import PartitionSpec as P

MAXD = 16
LANES = 128
CHUNKS = 4
MESH = pl.DeviceIdType.MESH


def halves(table):
    high = table.astype(np.float32).astype(ml_dtypes.bfloat16)
    low = (table - high.astype(np.float64)).astype(np.float32).astype(ml_dtypes.bfloat16)
    return high, low


def tables(length, channels_total):
    wide = length // LANES
    half = wide // 2
    rows = np.arange(LANES)
    cols = np.arange(wide)
    outs = np.arange(half)
    first = 2 * np.pi * (rows[:, None] * rows[None, :] % LANES) / LANES
    one = np.concatenate([np.cos(first), -np.sin(first)], axis=0)
    turn = 2 * np.pi * (rows[:, None] * cols[None, :] % length) / length
    scale = channels_total ** -0.5 * length ** -0.5
    twist = np.stack([np.cos(turn), np.sin(turn)]) * scale
    second = 2 * np.pi * (cols[:, None] * outs[None, :] % wide) / wide
    c2, s2 = np.cos(second), np.sin(second)
    real = np.concatenate([c2, s2], axis=0)
    imag = np.concatenate([-s2, c2], axis=0)
    two = np.concatenate([real, real, imag, imag], axis=1)
    one = np.concatenate(halves(one), axis=1)
    two = np.stack(halves(two))
    return jnp.asarray(one), jnp.asarray(twist, jnp.float32), jnp.asarray(two)


def split(x):
    high = x.astype(jnp.bfloat16)
    return high, (x - high.astype(jnp.float32)).astype(jnp.bfloat16)


def dot(a, b):
    return jnp.dot(a, b, preferred_element_type=jnp.float32)


def kernel(
    sizes,
    fb_ref, delay_hbm, bank_hbm, accel_hbm, one_hbm, twist_hbm, two_hbm,
    peaks_ref, energy_ref,
    delay_ref, xbuf, picked, acc, early, late, early_in, late_in, grid_ref,
    bank_ref, accel_ref, one_ref, twist_ref, two_ref, tmat,
    lsem, fsem, tsem, early_out_sem, early_in_sem, late_out_sem, late_in_sem,
):
    fft, xs, cores, dms, blocks = sizes
    chan = xs * cores
    cut = blocks // 2 + MAXD
    f = lax.axis_index("fft")
    c = lax.axis_index("chan")
    x, core = c // cores, c % cores
    columns = fb_ref.shape[1]
    chunk = columns // CHUNKS
    count = fft * chan
    partners = [
        (g, s, k) for g in range(fft) for s in range(xs) for k in range(cores) if (g, s, k) != (0, 0, 0)
    ]
    far_first = sorted(partners, key=lambda p: (-min(p[0], fft - p[0]) - p[1], -p[2]))

    def fetch(i):
        return pltpu.make_async_copy(
            fb_ref.at[:, i * chunk:(i + 1) * chunk], xbuf.at[i], fsem.at[i]
        )

    loads = [
        pltpu.make_async_copy(a, b, tsem.at[i])
        for i, (a, b) in enumerate(
            [
                (bank_hbm, bank_ref), (accel_hbm, accel_ref), (one_hbm, one_ref),
                (twist_hbm, twist_ref), (two_hbm, two_ref),
            ]
        )
    ]
    lags = pltpu.make_async_copy(delay_hbm, delay_ref, lsem)
    lags.start()
    order = list(range(CHUNKS))[::-1]
    for n, i in enumerate(order):
        fetch(i).start(priority=min(n, 1))

    def place(p):
        g, s, k = p
        return (f + g) % fft, ((x + s) % xs) * cores + (core + k) % cores

    barrier = pltpu.get_barrier_semaphore()
    for p in partners:
        g, d = place(p)
        pl.semaphore_signal(barrier, inc=1, device_id={"fft": g, "chan": d}, device_id_type=MESH)

    acc[...] = jnp.zeros_like(acc)
    lags.wait()
    lag = delay_ref[...]
    for o in range(MAXD):
        picked[(MAXD - 1 - o) * dms:(MAXD - o) * dms, :] = jnp.where(lag == o, 1.0, 0.0).astype(
            jnp.bfloat16
        )

    def slot(p):
        return (p[0] * xs + p[1]) * cores + p[2]

    def send(p, out, into, out_sem, in_sem):
        g, d = place(p)
        return pltpu.make_async_remote_copy(
            out.at[g * chan + d], into.at[slot(p)], out_sem, in_sem,
            device_id={"fft": g, "chan": d}, device_id_type=MESH,
        )

    def send_early(p):
        return send(p, early, early_in, early_out_sem, early_in_sem)

    def send_late(p):
        return send(p, late, late_in, late_out_sem, late_in_sem)

    def everything(ref, sem):
        part = ref.at[pl.ds(1, count - 1)]
        return pltpu.make_async_copy(part, part, sem)

    for n, i in enumerate(order):
        fetch(i).wait()
        for b in range(chunk // 256):
            y = dot(picked[...], xbuf[i, :, b * 256:(b + 1) * 256])
            for h in range(2):
                row = (i * (chunk // LANES) + 2 * b + h + 1) * dms
                acc[row:row + MAXD * dms, :] += y[:, h * LANES:(h + 1) * LANES]
        if n == CHUNKS // 2 - 1:
            for d in range(count):
                early[d] = acc[pl.ds(cut * dms + d, blocks + MAXD - cut, stride=dms), :].astype(
                    jnp.bfloat16
                )
            pl.semaphore_wait(barrier, len(partners))
            for p in far_first:
                send_early(p).start()
    for d in range(count):
        late[d] = acc[pl.ds(d, cut, stride=dms), :].astype(jnp.bfloat16)
    for p in far_first:
        send_late(p).start()
    for load in loads:
        load.start()

    loads[0].wait()
    loads[1].wait()
    accel = accel_ref[...]
    bank = bank_ref.shape[2]
    accels = accel.shape[1]
    taps = bank_ref.shape[1]
    chosen = jnp.where(
        lax.broadcasted_iota(jnp.int32, (bank, accels), 0) == accel, 1.0, 0.0
    ).astype(jnp.bfloat16)
    rows = []
    for part_index in range(2):
        row = dot(bank_ref[part_index], chosen)
        row = jnp.concatenate([row, jnp.zeros((LANES - taps, accels), jnp.float32)], axis=0)
        rows.append(row.T)
    for kk in range(LANES // 2):
        for part_index in range(2):
            shifted = pltpu.roll(rows[part_index], kk, 1) if kk else rows[part_index]
            tmat[kk * accels:(kk + 1) * accels, part_index * LANES:(part_index + 1) * LANES] = (
                shifted.astype(jnp.bfloat16)
            )
    for load in loads[2:]:
        load.wait()

    own = f * chan + c
    everything(early_in, early_in_sem).wait()
    everything(late_in, late_in_sem).wait()

    def gathered(z, own_ref, in_ref, lo, hi):
        base = ((f + fft - z) % fft) * chan
        total = None
        for k in range(chan):
            value = in_ref[base + k, lo:hi, :].astype(jnp.float32)
            total = value if total is None else total + value
        return total

    early_in[0] = early[own]
    late_in[0] = late[own]
    for z in range(fft):
        body = gathered(z, late, late_in, MAXD, cut)
        if z + 1 < fft:
            tail = gathered(z, early, early_in, 0, blocks + MAXD - cut)
            lead = gathered(z + 1, late, late_in, 0, MAXD)
            gap = tail.shape[0] - MAXD
            if gap:
                tail = jnp.concatenate([tail[:gap], tail[gap:] + lead], axis=0)
            else:
                tail = tail + lead
        else:
            tail = gathered(z, early, early_in, 0, blocks + MAXD - cut)
        grid_ref[z * blocks:z * blocks + cut - MAXD, :] = body
        grid_ref[z * blocks + cut - MAXD:(z + 1) * blocks, :] = tail

    wide = grid_ref.shape[0]
    half = wide // 2
    data = grid_ref[...] if wide == LANES else grid_ref[...].reshape(LANES, wide)
    high, low = split(data)
    both = jnp.concatenate(
        [
            jnp.concatenate([high, low], axis=1),
            jnp.concatenate([high, jnp.zeros_like(low)], axis=1),
        ],
        axis=0,
    )
    mixed = dot(one_ref[...], both)
    mixed = mixed[:, :wide] + mixed[:, wide:]
    re, im = mixed[:LANES], mixed[LANES:]
    tc, ts = twist_ref[0], twist_ref[1]
    turned = jnp.concatenate([re * tc + im * ts, im * tc - re * ts], axis=1)
    high, low = split(turned)
    spec = dot(high, two_ref[0]) + dot(low, two_ref[0]) + dot(high, two_ref[1])

    lane = lax.broadcasted_iota(jnp.int32, (16, 2 * half), 1)
    low64 = lax.broadcasted_iota(jnp.int32, (64, 2 * half), 1) < half
    low16 = lane < half
    sides = []
    square = jnp.zeros((LANES, 2 * half), jnp.float32)
    for part_index in range(2):
        o = spec[:, part_index * 2 * half:(part_index + 1) * 2 * half]
        square = square + o * o
        before = jnp.where(lane == 0, 0.0, pltpu.roll(o[LANES - 16:], 1, 1))
        after = jnp.where(lane == 2 * half - 1, 0.0, pltpu.roll(o[:16], 2 * half - 1, 1))
        sides.append(
            jnp.concatenate(
                [
                    jnp.where(low16, before, o[48:64]),
                    jnp.where(low64, o[:64], o[64:]),
                    jnp.where(low16, o[64:80], after),
                    jnp.zeros((32, 2 * half), jnp.float32),
                ],
                axis=0,
            ).astype(jnp.bfloat16)
        )
    energy_ref[0] = jnp.sum(square) * 0.5
    sr, si = sides
    window = jnp.concatenate(
        [jnp.concatenate([sr, si], axis=1), jnp.concatenate([-si, sr], axis=1)], axis=0
    )
    best = jnp.zeros((accels, 2 * half), jnp.float32)
    group = 8
    for g in range(LANES // 2 // group):
        out = dot(tmat[g * group * accels:(g + 1) * group * accels, :], window)
        for kk in range(group):
            rr = out[kk * accels:(kk + 1) * accels, :2 * half]
            ii = out[kk * accels:(kk + 1) * accels, 2 * half:]
            best = jnp.maximum(best, rr * rr + ii * ii)
    best = jnp.maximum(best, pltpu.roll(best, half, 1))
    peaks_ref[0] = best[:, :half]
    everything(early, early_out_sem).wait()
    everything(late, late_out_sem).wait()


def solution(mesh):
    fft, chan = mesh.shape["fft"], mesh.shape["chan"]
    cores = 2
    xs = chan // cores

    def body(filterbank, delays, template_bank, accel_index):
        channels, samples = filterbank.shape
        dms = delays.shape[1]
        accels = accel_index.shape[0]
        length = samples * fft
        blocks = samples // LANES
        wide = length // LANES
        cut = blocks // 2 + MAXD
        rest = blocks + MAXD - cut
        one, twist, two = tables(length, channels * chan)
        bank = template_bank.transpose(0, 2, 1)
        accel = accel_index[None, :]
        f32, bf16 = jnp.float32, jnp.bfloat16
        dma = pltpu.SemaphoreType.DMA
        hbm = pl.BlockSpec(memory_space=pltpu.HBM)
        vmem = pl.BlockSpec(memory_space=pltpu.VMEM)

        def like(a):
            return pltpu.VMEM(a.shape, a.dtype)

        return pl.pallas_call(
            functools.partial(kernel, (fft, xs, cores, dms, blocks)),
            out_shape=(
                pltpu.VMEM((1, accels, wide // 2), f32),
                pltpu.SMEM((1,), f32),
            ),
            in_specs=[hbm] * 7,
            out_specs=(vmem, pl.BlockSpec(memory_space=pltpu.SMEM)),
            scratch_shapes=[
                pltpu.VMEM((dms, channels), jnp.int32),
                pltpu.VMEM((CHUNKS, channels, samples // CHUNKS), bf16),
                pltpu.VMEM((MAXD * dms, channels), bf16),
                pltpu.VMEM(((blocks + MAXD) * dms, LANES), f32),
                pltpu.VMEM((dms, rest, LANES), bf16),
                pltpu.VMEM((dms, cut, LANES), bf16),
                pltpu.VMEM((dms, rest, LANES), bf16),
                pltpu.VMEM((dms, cut, LANES), bf16),
                pltpu.VMEM((wide, LANES), f32),
                like(bank), like(accel), like(one), like(twist), like(two),
                pltpu.VMEM((LANES // 2 * accels, 2 * LANES), bf16),
                dma, dma((CHUNKS,)), dma((5,)), dma, dma, dma, dma,
            ],
            compiler_params=pltpu.CompilerParams(
                collective_id=0, has_side_effects=True, vmem_limit_bytes=56 * 2 ** 20
            ),
            name="search",
        )(filterbank, delays.T, bank, accel, one, twist, two)

    in_specs = (P(("beam", "chan"), "fft"), P("chan", None), P(), P())
    out_specs = (P(("beam", "fft", "chan"), None, None), P(("beam", "fft", "chan")))
    return jax.shard_map(body, mesh=mesh, in_specs=in_specs, out_specs=out_specs, check_vma=False)
```

```python
import functools

import jax
import jax.numpy as jnp
import ml_dtypes
import numpy as np
from jax import lax
from jax.experimental import pallas as pl
from jax.experimental.pallas import tpu as pltpu
from jax.sharding import PartitionSpec as P

MAXD = 16
LANES = 128
CHUNKS = 4
MESH = pl.DeviceIdType.MESH


def halves(table):
    high = table.astype(np.float32).astype(ml_dtypes.bfloat16)
    low = (table - high.astype(np.float64)).astype(np.float32).astype(ml_dtypes.bfloat16)
    return high, low


def tables(length, channels_total):
    wide = length // LANES
    half = wide // 2
    rows = np.arange(LANES)
    cols = np.arange(wide)
    outs = np.arange(half)
    first = 2 * np.pi * (rows[:, None] * rows[None, :] % LANES) / LANES
    one = np.concatenate([np.cos(first), -np.sin(first)], axis=0)
    turn = 2 * np.pi * (rows[:, None] * cols[None, :] % length) / length
    scale = channels_total ** -0.5 * length ** -0.5
    twist = np.stack([np.cos(turn), np.sin(turn)]) * scale
    second = 2 * np.pi * (cols[:, None] * outs[None, :] % wide) / wide
    c2, s2 = np.cos(second), np.sin(second)
    real = np.concatenate([c2, s2], axis=0)
    imag = np.concatenate([-s2, c2], axis=0)
    two = np.concatenate([real, real, imag, imag], axis=1)
    one = np.concatenate(halves(one), axis=1)
    two = np.stack(halves(two))
    return jnp.asarray(one), jnp.asarray(twist, jnp.float32), jnp.asarray(two)


def split(x):
    high = x.astype(jnp.bfloat16)
    return high, (x - high.astype(jnp.float32)).astype(jnp.bfloat16)


def dot(a, b):
    return jnp.dot(a, b, preferred_element_type=jnp.float32)


def kernel(
    sizes,
    fb_ref, delay_hbm, bank_hbm, accel_hbm, one_hbm, twist_hbm, two_hbm,
    peaks_ref, energy_ref,
    delay_ref, xbuf, picked, acc, early, late, early_in, late_in, grid_ref,
    bank_ref, accel_ref, one_ref, twist_ref, two_ref, tmat,
    lsem, fsem, tsem, early_out_sem, early_in_sem, late_out_sem, late_in_sem,
):
    fft, xs, cores, dms, blocks = sizes
    chan = xs * cores
    cut = blocks // 2 + MAXD
    f = lax.axis_index("fft")
    c = lax.axis_index("chan")
    x, core = c // cores, c % cores
    columns = fb_ref.shape[1]
    chunk = columns // CHUNKS
    count = fft * chan
    partners = [
        (g, s, k) for g in range(fft) for s in range(xs) for k in range(cores) if (g, s, k) != (0, 0, 0)
    ]
    far_first = sorted(partners, key=lambda p: (-min(p[0], fft - p[0]) - p[1], -p[2]))

    def fetch(i):
        return pltpu.make_async_copy(
            fb_ref.at[:, i * chunk:(i + 1) * chunk], xbuf.at[i], fsem.at[i]
        )

    loads = [
        pltpu.make_async_copy(a, b, tsem.at[i])
        for i, (a, b) in enumerate(
            [
                (bank_hbm, bank_ref), (accel_hbm, accel_ref), (one_hbm, one_ref),
                (twist_hbm, twist_ref), (two_hbm, two_ref),
            ]
        )
    ]
    lags = pltpu.make_async_copy(delay_hbm, delay_ref, lsem)
    lags.start()
    order = list(range(CHUNKS))[::-1]
    for n, i in enumerate(order):
        fetch(i).start(priority=min(n, 1))

    def place(p):
        g, s, k = p
        return (f + g) % fft, ((x + s) % xs) * cores + (core + k) % cores

    barrier = pltpu.get_barrier_semaphore()
    for p in partners:
        g, d = place(p)
        pl.semaphore_signal(barrier, inc=1, device_id={"fft": g, "chan": d}, device_id_type=MESH)

    acc[...] = jnp.zeros_like(acc)
    lags.wait()
    lag = delay_ref[...]
    for o in range(MAXD):
        picked[(MAXD - 1 - o) * dms:(MAXD - o) * dms, :] = jnp.where(lag == o, 1.0, 0.0).astype(
            jnp.bfloat16
        )

    def slot(p):
        return (p[0] * xs + p[1]) * cores + p[2]

    def send(p, out, into, out_sem, in_sem):
        g, d = place(p)
        return pltpu.make_async_remote_copy(
            out.at[g * chan + d], into.at[slot(p)], out_sem, in_sem,
            device_id={"fft": g, "chan": d}, device_id_type=MESH,
        )

    def send_early(p):
        return send(p, early, early_in, early_out_sem, early_in_sem)

    def send_late(p):
        return send(p, late, late_in, late_out_sem, late_in_sem)

    def everything(ref, sem):
        part = ref.at[pl.ds(1, count - 1)]
        return pltpu.make_async_copy(part, part, sem)

    for n, i in enumerate(order):
        fetch(i).wait()
        for b in range(chunk // 256):
            y = dot(picked[...], xbuf[i, :, b * 256:(b + 1) * 256])
            for h in range(2):
                row = (i * (chunk // LANES) + 2 * b + h + 1) * dms
                acc[row:row + MAXD * dms, :] += y[:, h * LANES:(h + 1) * LANES]
        if n == CHUNKS // 2 - 1:
            for d in range(count):
                early[d] = acc[pl.ds(cut * dms + d, blocks + MAXD - cut, stride=dms), :].astype(
                    jnp.bfloat16
                )
            pl.semaphore_wait(barrier, len(partners))
            for p in far_first:
                send_early(p).start()
    for d in range(count):
        late[d] = acc[pl.ds(d, cut, stride=dms), :].astype(jnp.bfloat16)
    for p in far_first:
        send_late(p).start()
    for load in loads:
        load.start()

    loads[0].wait()
    loads[1].wait()
    accel = accel_ref[...]
    bank = bank_ref.shape[2]
    accels = accel.shape[1]
    taps = bank_ref.shape[1]
    chosen = jnp.where(
        lax.broadcasted_iota(jnp.int32, (bank, accels), 0) == accel, 1.0, 0.0
    ).astype(jnp.bfloat16)
    rows = []
    for part_index in range(2):
        row = dot(bank_ref[part_index], chosen)
        row = jnp.concatenate([row, jnp.zeros((LANES - taps, accels), jnp.float32)], axis=0)
        rows.append(row.T)
    for kk in range(LANES // 2):
        for part_index in range(2):
            shifted = pltpu.roll(rows[part_index], kk, 1) if kk else rows[part_index]
            tmat[kk * accels:(kk + 1) * accels, part_index * LANES:(part_index + 1) * LANES] = (
                shifted.astype(jnp.bfloat16)
            )
    for load in loads[2:]:
        load.wait()

    own = f * chan + c
    everything(early_in, early_in_sem).wait()
    everything(late_in, late_in_sem).wait()

    def gathered(z, own_ref, in_ref, lo, hi):
        base = ((f + fft - z) % fft) * chan
        total = None
        for k in range(chan):
            value = in_ref[base + k, lo:hi, :].astype(jnp.float32)
            total = value if total is None else total + value
        return total

    early_in[0] = early[own]
    late_in[0] = late[own]
    for z in range(fft):
        body = gathered(z, late, late_in, MAXD, cut)
        if z + 1 < fft:
            tail = gathered(z, early, early_in, 0, blocks + MAXD - cut)
            lead = gathered(z + 1, late, late_in, 0, MAXD)
            gap = tail.shape[0] - MAXD
            if gap:
                tail = jnp.concatenate([tail[:gap], tail[gap:] + lead], axis=0)
            else:
                tail = tail + lead
        else:
            tail = gathered(z, early, early_in, 0, blocks + MAXD - cut)
        grid_ref[z * blocks:z * blocks + cut - MAXD, :] = body
        grid_ref[z * blocks + cut - MAXD:(z + 1) * blocks, :] = tail

    wide = grid_ref.shape[0]
    half = wide // 2
    data = grid_ref[...] if wide == LANES else grid_ref[...].reshape(LANES, wide)
    high, low = split(data)
    both = jnp.concatenate(
        [
            jnp.concatenate([high, low], axis=1),
            jnp.concatenate([high, jnp.zeros_like(low)], axis=1),
        ],
        axis=0,
    )
    mixed = dot(one_ref[...], both)
    mixed = mixed[:, :wide] + mixed[:, wide:]
    re, im = mixed[:LANES], mixed[LANES:]
    tc, ts = twist_ref[0], twist_ref[1]
    turned = jnp.concatenate([re * tc + im * ts, im * tc - re * ts], axis=1)
    high, low = split(turned)
    spec = dot(high, two_ref[0]) + dot(low, two_ref[0]) + dot(high, two_ref[1])

    lane = lax.broadcasted_iota(jnp.int32, (16, 2 * half), 1)
    low64 = lax.broadcasted_iota(jnp.int32, (64, 2 * half), 1) < half
    low16 = lane < half
    sides = []
    square = jnp.zeros((LANES, 2 * half), jnp.float32)
    for part_index in range(2):
        o = spec[:, part_index * 2 * half:(part_index + 1) * 2 * half]
        square = square + o * o
        before = jnp.where(lane == 0, 0.0, pltpu.roll(o[LANES - 16:], 1, 1))
        after = jnp.where(lane == 2 * half - 1, 0.0, pltpu.roll(o[:16], 2 * half - 1, 1))
        sides.append(
            jnp.concatenate(
                [
                    jnp.where(low16, before, o[48:64]),
                    jnp.where(low64, o[:64], o[64:]),
                    jnp.where(low16, o[64:80], after),
                    jnp.zeros((32, 2 * half), jnp.float32),
                ],
                axis=0,
            ).astype(jnp.bfloat16)
        )
    energy_ref[0] = jnp.sum(square) * 0.5
    sr, si = sides
    window = jnp.concatenate(
        [jnp.concatenate([sr, si], axis=1), jnp.concatenate([-si, sr], axis=1)], axis=0
    )
    best = jnp.zeros((accels, 2 * half), jnp.float32)
    group = 8
    for g in range(LANES // 2 // group):
        out = dot(tmat[g * group * accels:(g + 1) * group * accels, :], window)
        for kk in range(group):
            rr = out[kk * accels:(kk + 1) * accels, :2 * half]
            ii = out[kk * accels:(kk + 1) * accels, 2 * half:]
            best = jnp.maximum(best, rr * rr + ii * ii)
    best = jnp.maximum(best, pltpu.roll(best, half, 1))
    peaks_ref[0] = best[:, :half]
    everything(early, early_out_sem).wait()
    everything(late, late_out_sem).wait()


def finish(found_ref, total_ref, peaks_ref, energy_ref):
    peaks_ref[...] = found_ref[...]
    energy_ref[0] = total_ref[0]


def solution(mesh):
    fft, chan = mesh.shape["fft"], mesh.shape["chan"]
    cores = 2
    xs = chan // cores

    def body(filterbank, delays, template_bank, accel_index):
        channels, samples = filterbank.shape
        dms = delays.shape[1]
        accels = accel_index.shape[0]
        length = samples * fft
        blocks = samples // LANES
        wide = length // LANES
        cut = blocks // 2 + MAXD
        rest = blocks + MAXD - cut
        one, twist, two = tables(length, channels * chan)
        bank = template_bank.transpose(0, 2, 1)
        accel = accel_index[None, :]
        f32, bf16 = jnp.float32, jnp.bfloat16
        dma = pltpu.SemaphoreType.DMA
        hbm = pl.BlockSpec(memory_space=pltpu.HBM)
        vmem = pl.BlockSpec(memory_space=pltpu.VMEM)

        def like(a):
            return pltpu.VMEM(a.shape, a.dtype)

        found, total = pl.pallas_call(
            functools.partial(kernel, (fft, xs, cores, dms, blocks)),
            out_shape=(
                pltpu.VMEM((1, accels, wide // 2), f32),
                pltpu.SMEM((1,), f32),
            ),
            in_specs=[hbm] * 7,
            out_specs=(vmem, pl.BlockSpec(memory_space=pltpu.SMEM)),
            scratch_shapes=[
                pltpu.VMEM((dms, channels), jnp.int32),
                pltpu.VMEM((CHUNKS, channels, samples // CHUNKS), bf16),
                pltpu.VMEM((MAXD * dms, channels), bf16),
                pltpu.VMEM(((blocks + MAXD) * dms, LANES), f32),
                pltpu.VMEM((dms, rest, LANES), bf16),
                pltpu.VMEM((dms, cut, LANES), bf16),
                pltpu.VMEM((dms, rest, LANES), bf16),
                pltpu.VMEM((dms, cut, LANES), bf16),
                pltpu.VMEM((wide, LANES), f32),
                like(bank), like(accel), like(one), like(twist), like(two),
                pltpu.VMEM((LANES // 2 * accels, 2 * LANES), bf16),
                dma, dma((CHUNKS,)), dma((5,)), dma, dma, dma, dma,
            ],
            compiler_params=pltpu.CompilerParams(
                collective_id=0, has_side_effects=True, vmem_limit_bytes=56 * 2 ** 20
            ),
            name="search",
        )(filterbank, delays.T, bank, accel, one, twist, two)

        return pl.pallas_call(
            finish,
            out_shape=(
                jax.ShapeDtypeStruct(found.shape, f32),
                jax.ShapeDtypeStruct(total.shape, f32),
            ),
            in_specs=[vmem, pl.BlockSpec(memory_space=pltpu.SMEM)],
            out_specs=(vmem, pl.BlockSpec(memory_space=pltpu.SMEM)),
            name="finish",
        )(pltpu.with_memory_space_constraint(found, pltpu.VMEM), pltpu.with_memory_space_constraint(total, pltpu.SMEM))

    in_specs = (P(("beam", "chan"), "fft"), P("chan", None), P(), P())
    out_specs = (P(("beam", "fft", "chan"), None, None), P(("beam", "fft", "chan")))
    return jax.shard_map(body, mesh=mesh, in_specs=in_specs, out_specs=out_specs, check_vma=False)
```

```python
import functools

import jax
import jax.numpy as jnp
import ml_dtypes
import numpy as np
from jax import lax
from jax.experimental import pallas as pl
from jax.experimental.pallas import tpu as pltpu
from jax.sharding import PartitionSpec as P

MAXD = 16
LANES = 128
SEGMENTS = ((1, 0), (1, 1), (1, 1), (1, 1))
MESH = pl.DeviceIdType.MESH


def halves(table):
    high = table.astype(np.float32).astype(ml_dtypes.bfloat16)
    low = (table - high.astype(np.float64)).astype(np.float32).astype(ml_dtypes.bfloat16)
    return high, low


def tables(length, channels_total):
    wide = length // LANES
    half = wide // 2
    rows = np.arange(LANES)
    cols = np.arange(wide)
    outs = np.arange(half)
    first = 2 * np.pi * (rows[:, None] * rows[None, :] % LANES) / LANES
    one = np.concatenate([np.cos(first), -np.sin(first)], axis=0)
    turn = 2 * np.pi * (rows[:, None] * cols[None, :] % length) / length
    scale = channels_total ** -0.5 * length ** -0.5
    twist = np.stack([np.cos(turn), np.sin(turn)]) * scale
    second = 2 * np.pi * (cols[:, None] * outs[None, :] % wide) / wide
    c2, s2 = np.cos(second), np.sin(second)
    real = np.concatenate([c2, s2], axis=0)
    imag = np.concatenate([-s2, c2], axis=0)
    two = np.concatenate([real, real, imag, imag], axis=1)
    one = np.concatenate(halves(one), axis=1)
    two = np.stack(halves(two))
    return jnp.asarray(one), jnp.asarray(twist, jnp.float32), jnp.asarray(two)


def split(x):
    high = x.astype(jnp.bfloat16)
    return high, (x - high.astype(jnp.float32)).astype(jnp.bfloat16)


def dot(a, b):
    return jnp.dot(a, b, preferred_element_type=jnp.float32)


def kernel(
    sizes,
    fb_ref, delay_hbm, bank_hbm, accel_hbm, one_hbm, twist_hbm, two_hbm,
    peaks_ref, energy_ref,
    delay_ref, xbuf, picked, acc, early, late, early_in, late_in, grid_ref,
    bank_ref, accel_ref, one_ref, twist_ref, two_ref, tmat,
    lsem, fsem, tsem, early_out_sem, early_in_sem, late_out_sem, late_in_sem,
):
    fft, xs, cores, dms, blocks = sizes
    chan = xs * cores
    cut = blocks // 2 + MAXD
    f = lax.axis_index("fft")
    c = lax.axis_index("chan")
    x, core = c // cores, c % cores
    columns = fb_ref.shape[1]
    unit = columns // sum(n for n, _ in SEGMENTS)
    count = fft * chan
    partners = [
        (g, s, k) for g in range(fft) for s in range(xs) for k in range(cores) if (g, s, k) != (0, 0, 0)
    ]
    far_first = sorted(partners, key=lambda p: (-min(p[0], fft - p[0]) - p[1], -p[2]))

    ends = [columns - unit * sum(n for n, _ in SEGMENTS[:i]) for i in range(len(SEGMENTS))]
    starts = ends[1:] + [0]

    def fetch(i):
        return pltpu.make_async_copy(
            fb_ref.at[:, starts[i]:ends[i]], xbuf.at[:, starts[i]:ends[i]], fsem.at[i]
        )

    loads = [
        pltpu.make_async_copy(a, b, tsem.at[i])
        for i, (a, b) in enumerate(
            [
                (bank_hbm, bank_ref), (accel_hbm, accel_ref), (one_hbm, one_ref),
                (twist_hbm, twist_ref), (two_hbm, two_ref),
            ]
        )
    ]
    lags = pltpu.make_async_copy(delay_hbm, delay_ref, lsem)
    lags.start()
    for i, (_, priority) in enumerate(SEGMENTS):
        fetch(i).start(priority=priority)

    def place(p):
        g, s, k = p
        return (f + g) % fft, ((x + s) % xs) * cores + (core + k) % cores

    barrier = pltpu.get_barrier_semaphore()
    for p in partners:
        g, d = place(p)
        pl.semaphore_signal(barrier, inc=1, device_id={"fft": g, "chan": d}, device_id_type=MESH)

    acc[...] = jnp.zeros_like(acc)
    lags.wait()
    lag = delay_ref[...]
    for o in range(MAXD):
        picked[(MAXD - 1 - o) * dms:(MAXD - o) * dms, :] = jnp.where(lag == o, 1.0, 0.0).astype(
            jnp.bfloat16
        )

    def slot(p):
        return (p[0] * xs + p[1]) * cores + p[2]

    def send(p, out, into, out_sem, in_sem):
        g, d = place(p)
        return pltpu.make_async_remote_copy(
            out.at[g * chan + d], into.at[slot(p)], out_sem, in_sem,
            device_id={"fft": g, "chan": d}, device_id_type=MESH,
        )

    def send_early(p):
        return send(p, early, early_in, early_out_sem, early_in_sem)

    def send_late(p):
        return send(p, late, late_in, late_out_sem, late_in_sem)

    def everything(ref, sem):
        part = ref.at[pl.ds(1, count - 1)]
        return pltpu.make_async_copy(part, part, sem)

    for i in range(len(SEGMENTS)):
        fetch(i).wait()
        for b in range(starts[i] // 256, ends[i] // 256):
            y = dot(picked[...], xbuf[:, b * 256:(b + 1) * 256])
            for h in range(2):
                row = (2 * b + h + 1) * dms
                acc[row:row + MAXD * dms, :] += y[:, h * LANES:(h + 1) * LANES]
        if starts[i] == columns // 2:
            for d in range(count):
                early[d] = acc[pl.ds(cut * dms + d, blocks + MAXD - cut, stride=dms), :].astype(
                    jnp.bfloat16
                )
            pl.semaphore_wait(barrier, len(partners))
            for p in far_first:
                send_early(p).start()
    for a in range(fft):
        for b in range(chan):
            d = a * chan + b
            late[d] = acc[pl.ds(d, cut, stride=dms), :].astype(jnp.bfloat16)
            xa, ka = b // cores, b % cores

            @pl.when((a != f) | (b != c))
            def _():
                send_late(
                    ((a - f + fft) % fft, (xa - x + xs) % xs, (ka - core + cores) % cores)
                ).start()
    for load in loads:
        load.start()

    loads[0].wait()
    loads[1].wait()
    accel = accel_ref[...]
    bank = bank_ref.shape[2]
    accels = accel.shape[1]
    taps = bank_ref.shape[1]
    chosen = jnp.where(
        lax.broadcasted_iota(jnp.int32, (bank, accels), 0) == accel, 1.0, 0.0
    ).astype(jnp.bfloat16)
    rows = []
    for part_index in range(2):
        row = dot(bank_ref[part_index], chosen)
        row = jnp.concatenate([row, jnp.zeros((LANES - taps, accels), jnp.float32)], axis=0)
        rows.append(row.T)
    for kk in range(LANES // 2):
        for part_index in range(2):
            shifted = pltpu.roll(rows[part_index], kk, 1) if kk else rows[part_index]
            tmat[kk * accels:(kk + 1) * accels, part_index * LANES:(part_index + 1) * LANES] = (
                shifted.astype(jnp.bfloat16)
            )
    for load in loads[2:]:
        load.wait()

    own = f * chan + c
    everything(early_in, early_in_sem).wait()
    everything(late_in, late_in_sem).wait()

    def gathered(z, own_ref, in_ref, lo, hi):
        base = ((f + fft - z) % fft) * chan
        total = None
        for k in range(chan):
            value = in_ref[base + k, lo:hi, :].astype(jnp.float32)
            total = value if total is None else total + value
        return total

    early_in[0] = early[own]
    late_in[0] = late[own]
    for z in range(fft):
        body = gathered(z, late, late_in, MAXD, cut)
        if z + 1 < fft:
            tail = gathered(z, early, early_in, 0, blocks + MAXD - cut)
            lead = gathered(z + 1, late, late_in, 0, MAXD)
            gap = tail.shape[0] - MAXD
            if gap:
                tail = jnp.concatenate([tail[:gap], tail[gap:] + lead], axis=0)
            else:
                tail = tail + lead
        else:
            tail = gathered(z, early, early_in, 0, blocks + MAXD - cut)
        grid_ref[z * blocks:z * blocks + cut - MAXD, :] = body
        grid_ref[z * blocks + cut - MAXD:(z + 1) * blocks, :] = tail

    wide = grid_ref.shape[0]
    half = wide // 2
    data = grid_ref[...] if wide == LANES else grid_ref[...].reshape(LANES, wide)
    high, low = split(data)
    both = jnp.concatenate(
        [
            jnp.concatenate([high, low], axis=1),
            jnp.concatenate([high, jnp.zeros_like(low)], axis=1),
        ],
        axis=0,
    )
    mixed = dot(one_ref[...], both)
    mixed = mixed[:, :wide] + mixed[:, wide:]
    re, im = mixed[:LANES], mixed[LANES:]
    tc, ts = twist_ref[0], twist_ref[1]
    turned = jnp.concatenate([re * tc + im * ts, im * tc - re * ts], axis=1)
    high, low = split(turned)
    spec = dot(high, two_ref[0]) + dot(low, two_ref[0]) + dot(high, two_ref[1])

    lane = lax.broadcasted_iota(jnp.int32, (16, 2 * half), 1)
    low64 = lax.broadcasted_iota(jnp.int32, (64, 2 * half), 1) < half
    low16 = lane < half
    sides = []
    square = jnp.zeros((LANES, 2 * half), jnp.float32)
    for part_index in range(2):
        o = spec[:, part_index * 2 * half:(part_index + 1) * 2 * half]
        square = square + o * o
        before = jnp.where(lane == 0, 0.0, pltpu.roll(o[LANES - 16:], 1, 1))
        after = jnp.where(lane == 2 * half - 1, 0.0, pltpu.roll(o[:16], 2 * half - 1, 1))
        sides.append(
            jnp.concatenate(
                [
                    jnp.where(low16, before, o[48:64]),
                    jnp.where(low64, o[:64], o[64:]),
                    jnp.where(low16, o[64:80], after),
                    jnp.zeros((32, 2 * half), jnp.float32),
                ],
                axis=0,
            ).astype(jnp.bfloat16)
        )
    energy_ref[0] = jnp.sum(square) * 0.5
    sr, si = sides
    window = jnp.concatenate(
        [jnp.concatenate([sr, si], axis=1), jnp.concatenate([-si, sr], axis=1)], axis=0
    )
    best = jnp.zeros((accels, 2 * half), jnp.float32)
    group = 8
    for g in range(LANES // 2 // group):
        out = dot(tmat[g * group * accels:(g + 1) * group * accels, :], window)
        for kk in range(group):
            rr = out[kk * accels:(kk + 1) * accels, :2 * half]
            ii = out[kk * accels:(kk + 1) * accels, 2 * half:]
            best = jnp.maximum(best, rr * rr + ii * ii)
    best = jnp.maximum(best, pltpu.roll(best, half, 1))
    peaks_ref[0] = best[:, :half]
    everything(early, early_out_sem).wait()
    everything(late, late_out_sem).wait()


def finish(found_ref, total_ref, peaks_ref, energy_ref):
    peaks_ref[...] = found_ref[...]
    energy_ref[0] = total_ref[0]


def solution(mesh):
    fft, chan = mesh.shape["fft"], mesh.shape["chan"]
    cores = 2
    xs = chan // cores

    def body(filterbank, delays, template_bank, accel_index):
        channels, samples = filterbank.shape
        dms = delays.shape[1]
        accels = accel_index.shape[0]
        length = samples * fft
        blocks = samples // LANES
        wide = length // LANES
        cut = blocks // 2 + MAXD
        rest = blocks + MAXD - cut
        one, twist, two = tables(length, channels * chan)
        bank = template_bank.transpose(0, 2, 1)
        accel = accel_index[None, :]
        f32, bf16 = jnp.float32, jnp.bfloat16
        dma = pltpu.SemaphoreType.DMA
        hbm = pl.BlockSpec(memory_space=pltpu.HBM)
        vmem = pl.BlockSpec(memory_space=pltpu.VMEM)

        def like(a):
            return pltpu.VMEM(a.shape, a.dtype)

        found, total = pl.pallas_call(
            functools.partial(kernel, (fft, xs, cores, dms, blocks)),
            out_shape=(
                pltpu.VMEM((1, accels, wide // 2), f32),
                pltpu.SMEM((1,), f32),
            ),
            in_specs=[hbm] * 7,
            out_specs=(vmem, pl.BlockSpec(memory_space=pltpu.SMEM)),
            scratch_shapes=[
                pltpu.VMEM((dms, channels), jnp.int32),
                pltpu.VMEM((channels, samples), bf16),
                pltpu.VMEM((MAXD * dms, channels), bf16),
                pltpu.VMEM(((blocks + MAXD) * dms, LANES), f32),
                pltpu.VMEM((dms, rest, LANES), bf16),
                pltpu.VMEM((dms, cut, LANES), bf16),
                pltpu.VMEM((dms, rest, LANES), bf16),
                pltpu.VMEM((dms, cut, LANES), bf16),
                pltpu.VMEM((wide, LANES), f32),
                like(bank), like(accel), like(one), like(twist), like(two),
                pltpu.VMEM((LANES // 2 * accels, 2 * LANES), bf16),
                dma, dma((len(SEGMENTS),)), dma((5,)), dma, dma, dma, dma,
            ],
            compiler_params=pltpu.CompilerParams(
                collective_id=0, has_side_effects=True, vmem_limit_bytes=56 * 2 ** 20
            ),
            name="search",
        )(filterbank, delays.T, bank, accel, one, twist, two)

        return pl.pallas_call(
            finish,
            out_shape=(
                jax.ShapeDtypeStruct(found.shape, f32),
                jax.ShapeDtypeStruct(total.shape, f32),
            ),
            in_specs=[vmem, pl.BlockSpec(memory_space=pltpu.SMEM)],
            out_specs=(vmem, pl.BlockSpec(memory_space=pltpu.SMEM)),
            name="finish",
        )(pltpu.with_memory_space_constraint(found, pltpu.VMEM), pltpu.with_memory_space_constraint(total, pltpu.SMEM))

    in_specs = (P(("beam", "chan"), "fft"), P("chan", None), P(), P())
    out_specs = (P(("beam", "fft", "chan"), None, None), P(("beam", "fft", "chan")))
    return jax.shard_map(body, mesh=mesh, in_specs=in_specs, out_specs=out_specs, check_vma=False)
```

```python
import functools

import jax
import jax.numpy as jnp
import ml_dtypes
import numpy as np
from jax import lax
from jax.experimental import pallas as pl
from jax.experimental.pallas import tpu as pltpu
from jax.sharding import PartitionSpec as P

MAXD = 16
LANES = 128
PARTS = 2
SEGMENTS = ((1, 0), (1, 1), (1, 1), (1, 1))
MESH = pl.DeviceIdType.MESH


def halves(table):
    high = table.astype(np.float32).astype(ml_dtypes.bfloat16)
    low = (table - high.astype(np.float64)).astype(np.float32).astype(ml_dtypes.bfloat16)
    return high, low


def tables(length, channels_total):
    wide = length // LANES
    half = wide // 2
    rows = np.arange(LANES)
    cols = np.arange(wide)
    outs = np.arange(half)
    first = 2 * np.pi * (rows[:, None] * rows[None, :] % LANES) / LANES
    one = np.concatenate([np.cos(first), -np.sin(first)], axis=0)
    turn = 2 * np.pi * (rows[:, None] * cols[None, :] % length) / length
    scale = channels_total ** -0.5 * length ** -0.5
    twist = np.stack([np.cos(turn), np.sin(turn)]) * scale
    second = 2 * np.pi * (cols[:, None] * outs[None, :] % wide) / wide
    c2, s2 = np.cos(second), np.sin(second)
    real = np.concatenate([c2, s2], axis=0)
    imag = np.concatenate([-s2, c2], axis=0)
    two = np.concatenate([real, real, imag, imag], axis=1)
    one = np.concatenate(halves(one), axis=1)
    two = np.stack(halves(two))
    return jnp.asarray(one), jnp.asarray(twist, jnp.float32), jnp.asarray(two)


def split(x):
    high = x.astype(jnp.bfloat16)
    return high, (x - high.astype(jnp.float32)).astype(jnp.bfloat16)


def dot(a, b):
    return jnp.dot(a, b, preferred_element_type=jnp.float32)


def kernel(
    sizes,
    fb_ref, delay_hbm, bank_hbm, accel_hbm, one_hbm, twist_hbm, two_hbm,
    peaks_ref, energy_ref,
    delay_ref, xbuf, picked, acc, early, late, early_in, late_in, grid_ref,
    bank_ref, accel_ref, one_ref, twist_ref, two_ref, tmat,
    lsem, fsem, tsem, early_out_sem, early_in_sem, late_out_sem, late_in_sem,
):
    fft, xs, cores, dms, blocks = sizes
    chan = xs * cores
    cut = blocks // 2 + MAXD
    f = lax.axis_index("fft")
    c = lax.axis_index("chan")
    x, core = c // cores, c % cores
    columns = fb_ref.shape[1]
    unit = columns // sum(n for n, _ in SEGMENTS)
    count = fft * chan
    part = dms // PARTS
    partners = [
        (g, s, k) for g in range(fft) for s in range(xs) for k in range(cores) if (g, s, k) != (0, 0, 0)
    ]
    far_first = sorted(partners, key=lambda p: (-min(p[0], fft - p[0]) - p[1], -p[2]))

    ends = [columns - unit * sum(n for n, _ in SEGMENTS[:i]) for i in range(len(SEGMENTS))]
    starts = ends[1:] + [0]

    def fetch(i):
        return pltpu.make_async_copy(
            fb_ref.at[:, starts[i]:ends[i]], xbuf.at[:, starts[i]:ends[i]], fsem.at[i]
        )

    loads = [
        pltpu.make_async_copy(a, b, tsem.at[i])
        for i, (a, b) in enumerate(
            [
                (bank_hbm, bank_ref), (accel_hbm, accel_ref), (one_hbm, one_ref),
                (twist_hbm, twist_ref), (two_hbm, two_ref),
            ]
        )
    ]
    lags = pltpu.make_async_copy(delay_hbm, delay_ref, lsem)
    lags.start()
    for i, (_, priority) in enumerate(SEGMENTS):
        fetch(i).start(priority=priority)

    def place(p):
        g, s, k = p
        return (f + g) % fft, ((x + s) % xs) * cores + (core + k) % cores

    barrier = pltpu.get_barrier_semaphore()
    for p in partners:
        g, d = place(p)
        pl.semaphore_signal(barrier, inc=1, device_id={"fft": g, "chan": d}, device_id_type=MESH)

    acc[...] = jnp.zeros_like(acc)
    lags.wait()
    lag = delay_ref[...]
    for o in range(MAXD):
        row = (MAXD - 1 - o) * part
        hit = jnp.where(lag == o, 1.0, 0.0).astype(jnp.bfloat16)
        for q in range(PARTS):
            picked[q * MAXD * part + row:q * MAXD * part + row + part, :] = (
                hit[q * part:(q + 1) * part]
            )

    def slot(p):
        return (p[0] * xs + p[1]) * cores + p[2]

    def send(p, out, into, out_sem, in_sem):
        g, d = place(p)
        return pltpu.make_async_remote_copy(
            out.at[g * chan + d], into.at[slot(p)], out_sem, in_sem,
            device_id={"fft": g, "chan": d}, device_id_type=MESH,
        )

    def send_early(p):
        return send(p, early, early_in, early_out_sem, early_in_sem)

    def send_late(p):
        return send(p, late, late_in, late_out_sem, late_in_sem)

    def everything(ref, sem):
        slots = ref.at[pl.ds(1, count - 1)]
        return pltpu.make_async_copy(slots, slots, sem)

    def add(i, first, last):
        for b in range(starts[i] // 256, ends[i] // 256):
            y = dot(
                picked[first * MAXD * part:last * MAXD * part, :], xbuf[:, b * 256:(b + 1) * 256]
            )
            for q in range(first, last):
                for h in range(2):
                    row = (2 * b + h + 1) * part
                    acc[q, row:row + MAXD * part, :] += y[
                        (q - first) * MAXD * part:(q - first + 1) * MAXD * part,
                        h * LANES:(h + 1) * LANES,
                    ]

    def cut_out(d, lo, hi):
        q, r = d // part, d % part
        return acc[q, pl.ds(lo * part + r, hi - lo, stride=part), :].astype(jnp.bfloat16)

    def send_owner(d, send_one):
        a, b = d // chan, d % chan
        xa, ka = b // cores, b % cores

        @pl.when((a != f) | (b != c))
        def _():
            send_one(
                ((a - f + fft) % fft, (xa - x + xs) % xs, (ka - core + cores) % cores)
            ).start()

    for i in range(len(SEGMENTS) - 1):
        fetch(i).wait()
        add(i, 0, PARTS)
        if starts[i] == columns // 2:
            for d in range(count):
                early[d] = cut_out(d, cut, blocks + MAXD)
            pl.semaphore_wait(barrier, len(partners))
            for p in far_first:
                send_early(p).start()
    fetch(len(SEGMENTS) - 1).wait()
    for q in range(PARTS):
        add(len(SEGMENTS) - 1, q, q + 1)
        for d in range(q * part, (q + 1) * part):
            late[d] = cut_out(d, 0, cut)
            send_owner(d, send_late)
    for load in loads:
        load.start()

    loads[0].wait()
    loads[1].wait()
    accel = accel_ref[...]
    bank = bank_ref.shape[2]
    accels = accel.shape[1]
    taps = bank_ref.shape[1]
    chosen = jnp.where(
        lax.broadcasted_iota(jnp.int32, (bank, accels), 0) == accel, 1.0, 0.0
    ).astype(jnp.bfloat16)
    rows = []
    for part_index in range(2):
        row = dot(bank_ref[part_index], chosen)
        row = jnp.concatenate([row, jnp.zeros((LANES - taps, accels), jnp.float32)], axis=0)
        rows.append(row.T)
    for kk in range(LANES // 2):
        for part_index in range(2):
            shifted = pltpu.roll(rows[part_index], kk, 1) if kk else rows[part_index]
            tmat[kk * accels:(kk + 1) * accels, part_index * LANES:(part_index + 1) * LANES] = (
                shifted.astype(jnp.bfloat16)
            )
    for load in loads[2:]:
        load.wait()

    own = f * chan + c
    everything(early_in, early_in_sem).wait()
    everything(late_in, late_in_sem).wait()

    def gathered(z, own_ref, in_ref, lo, hi):
        base = ((f + fft - z) % fft) * chan
        total = None
        for k in range(chan):
            value = in_ref[base + k, lo:hi, :].astype(jnp.float32)
            total = value if total is None else total + value
        return total

    early_in[0] = early[own]
    late_in[0] = late[own]
    for z in range(fft):
        body = gathered(z, late, late_in, MAXD, cut)
        if z + 1 < fft:
            tail = gathered(z, early, early_in, 0, blocks + MAXD - cut)
            lead = gathered(z + 1, late, late_in, 0, MAXD)
            gap = tail.shape[0] - MAXD
            if gap:
                tail = jnp.concatenate([tail[:gap], tail[gap:] + lead], axis=0)
            else:
                tail = tail + lead
        else:
            tail = gathered(z, early, early_in, 0, blocks + MAXD - cut)
        grid_ref[z * blocks:z * blocks + cut - MAXD, :] = body
        grid_ref[z * blocks + cut - MAXD:(z + 1) * blocks, :] = tail

    wide = grid_ref.shape[0]
    half = wide // 2
    data = grid_ref[...] if wide == LANES else grid_ref[...].reshape(LANES, wide)
    high, low = split(data)
    both = jnp.concatenate(
        [
            jnp.concatenate([high, low], axis=1),
            jnp.concatenate([high, jnp.zeros_like(low)], axis=1),
        ],
        axis=0,
    )
    mixed = dot(one_ref[...], both)
    mixed = mixed[:, :wide] + mixed[:, wide:]
    re, im = mixed[:LANES], mixed[LANES:]
    tc, ts = twist_ref[0], twist_ref[1]
    turned = jnp.concatenate([re * tc + im * ts, im * tc - re * ts], axis=1)
    high, low = split(turned)
    spec = dot(high, two_ref[0]) + dot(low, two_ref[0]) + dot(high, two_ref[1])

    lane = lax.broadcasted_iota(jnp.int32, (16, 2 * half), 1)
    low64 = lax.broadcasted_iota(jnp.int32, (64, 2 * half), 1) < half
    low16 = lane < half
    sides = []
    square = jnp.zeros((LANES, 2 * half), jnp.float32)
    for part_index in range(2):
        o = spec[:, part_index * 2 * half:(part_index + 1) * 2 * half]
        square = square + o * o
        before = jnp.where(lane == 0, 0.0, pltpu.roll(o[LANES - 16:], 1, 1))
        after = jnp.where(lane == 2 * half - 1, 0.0, pltpu.roll(o[:16], 2 * half - 1, 1))
        sides.append(
            jnp.concatenate(
                [
                    jnp.where(low16, before, o[48:64]),
                    jnp.where(low64, o[:64], o[64:]),
                    jnp.where(low16, o[64:80], after),
                    jnp.zeros((32, 2 * half), jnp.float32),
                ],
                axis=0,
            ).astype(jnp.bfloat16)
        )
    energy_ref[0] = jnp.sum(square) * 0.5
    sr, si = sides
    window = jnp.concatenate(
        [jnp.concatenate([sr, si], axis=1), jnp.concatenate([-si, sr], axis=1)], axis=0
    )
    best = jnp.zeros((accels, 2 * half), jnp.float32)
    group = 8
    for g in range(LANES // 2 // group):
        out = dot(tmat[g * group * accels:(g + 1) * group * accels, :], window)
        for kk in range(group):
            rr = out[kk * accels:(kk + 1) * accels, :2 * half]
            ii = out[kk * accels:(kk + 1) * accels, 2 * half:]
            best = jnp.maximum(best, rr * rr + ii * ii)
    best = jnp.maximum(best, pltpu.roll(best, half, 1))
    peaks_ref[0] = best[:, :half]
    everything(early, early_out_sem).wait()
    everything(late, late_out_sem).wait()


def finish(found_ref, total_ref, peaks_ref, energy_ref):
    peaks_ref[...] = found_ref[...]
    energy_ref[0] = total_ref[0]


def solution(mesh):
    fft, chan = mesh.shape["fft"], mesh.shape["chan"]
    cores = 2
    xs = chan // cores

    def body(filterbank, delays, template_bank, accel_index):
        channels, samples = filterbank.shape
        dms = delays.shape[1]
        accels = accel_index.shape[0]
        length = samples * fft
        blocks = samples // LANES
        wide = length // LANES
        cut = blocks // 2 + MAXD
        rest = blocks + MAXD - cut
        one, twist, two = tables(length, channels * chan)
        bank = template_bank.transpose(0, 2, 1)
        accel = accel_index[None, :]
        f32, bf16 = jnp.float32, jnp.bfloat16
        dma = pltpu.SemaphoreType.DMA
        hbm = pl.BlockSpec(memory_space=pltpu.HBM)
        vmem = pl.BlockSpec(memory_space=pltpu.VMEM)

        def like(a):
            return pltpu.VMEM(a.shape, a.dtype)

        found, total = pl.pallas_call(
            functools.partial(kernel, (fft, xs, cores, dms, blocks)),
            out_shape=(
                pltpu.VMEM((1, accels, wide // 2), f32),
                pltpu.SMEM((1,), f32),
            ),
            in_specs=[hbm] * 7,
            out_specs=(vmem, pl.BlockSpec(memory_space=pltpu.SMEM)),
            scratch_shapes=[
                pltpu.VMEM((dms, channels), jnp.int32),
                pltpu.VMEM((channels, samples), bf16),
                pltpu.VMEM((MAXD * dms, channels), bf16),
                pltpu.VMEM((PARTS, (blocks + MAXD) * dms // PARTS, LANES), f32),
                pltpu.VMEM((dms, rest, LANES), bf16),
                pltpu.VMEM((dms, cut, LANES), bf16),
                pltpu.VMEM((dms, rest, LANES), bf16),
                pltpu.VMEM((dms, cut, LANES), bf16),
                pltpu.VMEM((wide, LANES), f32),
                like(bank), like(accel), like(one), like(twist), like(two),
                pltpu.VMEM((LANES // 2 * accels, 2 * LANES), bf16),
                dma, dma((len(SEGMENTS),)), dma((5,)), dma, dma, dma, dma,
            ],
            compiler_params=pltpu.CompilerParams(
                collective_id=0, has_side_effects=True, vmem_limit_bytes=56 * 2 ** 20
            ),
            name="search",
        )(filterbank, delays.T, bank, accel, one, twist, two)

        return pl.pallas_call(
            finish,
            out_shape=(
                jax.ShapeDtypeStruct(found.shape, f32),
                jax.ShapeDtypeStruct(total.shape, f32),
            ),
            in_specs=[vmem, pl.BlockSpec(memory_space=pltpu.SMEM)],
            out_specs=(vmem, pl.BlockSpec(memory_space=pltpu.SMEM)),
            name="finish",
        )(pltpu.with_memory_space_constraint(found, pltpu.VMEM), pltpu.with_memory_space_constraint(total, pltpu.SMEM))

    in_specs = (P(("beam", "chan"), "fft"), P("chan", None), P(), P())
    out_specs = (P(("beam", "fft", "chan"), None, None), P(("beam", "fft", "chan")))
    return jax.shard_map(body, mesh=mesh, in_specs=in_specs, out_specs=out_specs, check_vma=False)
```

```python
import functools

import jax
import jax.numpy as jnp
import ml_dtypes
import numpy as np
from jax import lax
from jax.experimental import pallas as pl
from jax.experimental.pallas import tpu as pltpu
from jax.sharding import PartitionSpec as P

MAXD = 16
LANES = 128
PARTS = 2
TOGETHER = 1
SEGMENTS = ((1, 0), (1, 1), (1, 1), (1, 1))
MESH = pl.DeviceIdType.MESH


def halves(table):
    high = table.astype(np.float32).astype(ml_dtypes.bfloat16)
    low = (table - high.astype(np.float64)).astype(np.float32).astype(ml_dtypes.bfloat16)
    return high, low


def tables(length, channels_total):
    wide = length // LANES
    half = wide // 2
    rows = np.arange(LANES)
    cols = np.arange(wide)
    outs = np.arange(half)
    first = 2 * np.pi * (rows[:, None] * rows[None, :] % LANES) / LANES
    one = np.concatenate([np.cos(first), -np.sin(first)], axis=0)
    turn = 2 * np.pi * (rows[:, None] * cols[None, :] % length) / length
    scale = channels_total ** -0.5 * length ** -0.5
    twist = np.stack([np.cos(turn), np.sin(turn)]) * scale
    second = 2 * np.pi * (cols[:, None] * outs[None, :] % wide) / wide
    c2, s2 = np.cos(second), np.sin(second)
    real = np.concatenate([c2, s2], axis=0)
    imag = np.concatenate([-s2, c2], axis=0)
    two = np.concatenate([real, real, imag, imag], axis=1)
    one = np.concatenate(halves(one), axis=1)
    two = np.stack(halves(two))
    return jnp.asarray(one), jnp.asarray(twist, jnp.float32), jnp.asarray(two)


def split(x):
    high = x.astype(jnp.bfloat16)
    return high, (x - high.astype(jnp.float32)).astype(jnp.bfloat16)


def dot(a, b):
    return jnp.dot(a, b, preferred_element_type=jnp.float32)


def kernel(
    sizes,
    fb_ref, delay_hbm, bank_hbm, accel_hbm, one_hbm, twist_hbm, two_hbm,
    peaks_ref, energy_ref,
    delay_ref, xbuf, picked, acc, early, late, early_in, late_in, grid_ref,
    bank_ref, accel_ref, one_ref, twist_ref, two_ref, tmat,
    lsem, fsem, tsem, early_out_sem, early_in_sem, late_out_sem, late_in_sem,
):
    fft, xs, cores, dms, blocks = sizes
    chan = xs * cores
    cut = blocks // 2 + MAXD
    f = lax.axis_index("fft")
    c = lax.axis_index("chan")
    x, core = c // cores, c % cores
    columns = fb_ref.shape[1]
    unit = columns // sum(n for n, _ in SEGMENTS)
    count = fft * chan
    part = dms // PARTS
    partners = [
        (g, s, k) for g in range(fft) for s in range(xs) for k in range(cores) if (g, s, k) != (0, 0, 0)
    ]
    far_first = sorted(partners, key=lambda p: (-min(p[0], fft - p[0]) - p[1], -p[2]))

    ends = [columns - unit * sum(n for n, _ in SEGMENTS[:i]) for i in range(len(SEGMENTS))]
    starts = ends[1:] + [0]

    def fetch(i):
        return pltpu.make_async_copy(
            fb_ref.at[:, starts[i]:ends[i]], xbuf.at[:, starts[i]:ends[i]], fsem.at[i]
        )

    loads = [
        pltpu.make_async_copy(a, b, tsem.at[i])
        for i, (a, b) in enumerate(
            [
                (bank_hbm, bank_ref), (accel_hbm, accel_ref), (one_hbm, one_ref),
                (twist_hbm, twist_ref), (two_hbm, two_ref),
            ]
        )
    ]
    lags = pltpu.make_async_copy(delay_hbm, delay_ref, lsem)
    lags.start()
    for i, (_, priority) in enumerate(SEGMENTS):
        fetch(i).start(priority=priority)

    def place(p):
        g, s, k = p
        return (f + g) % fft, ((x + s) % xs) * cores + (core + k) % cores

    barrier = pltpu.get_barrier_semaphore()
    for p in partners:
        g, d = place(p)
        pl.semaphore_signal(barrier, inc=1, device_id={"fft": g, "chan": d}, device_id_type=MESH)

    acc[...] = jnp.zeros_like(acc)
    lags.wait()
    lag = delay_ref[...]
    for o in range(MAXD):
        row = (MAXD - 1 - o) * part
        hit = jnp.where(lag == o, 1.0, 0.0).astype(jnp.bfloat16)
        for q in range(PARTS):
            picked[q * MAXD * part + row:q * MAXD * part + row + part, :] = (
                hit[q * part:(q + 1) * part]
            )

    def slot(p):
        return (p[0] * xs + p[1]) * cores + p[2]

    def send(p, out, into, out_sem, in_sem):
        g, d = place(p)
        return pltpu.make_async_remote_copy(
            out.at[g * chan + d], into.at[slot(p)], out_sem, in_sem,
            device_id={"fft": g, "chan": d}, device_id_type=MESH,
        )

    def send_early(p):
        return send(p, early, early_in, early_out_sem, early_in_sem)

    def send_late(p):
        return send(p, late, late_in, late_out_sem, late_in_sem)

    def everything(ref, sem):
        slots = ref.at[pl.ds(1, count - 1)]
        return pltpu.make_async_copy(slots, slots, sem)

    def add(i, first, last):
        for b in range(starts[i] // 256, ends[i] // 256):
            y = dot(
                picked[first * MAXD * part:last * MAXD * part, :], xbuf[:, b * 256:(b + 1) * 256]
            )
            for q in range(first, last):
                for h in range(2):
                    row = (2 * b + h + 1) * part
                    acc[q, row:row + MAXD * part, :] += y[
                        (q - first) * MAXD * part:(q - first + 1) * MAXD * part,
                        h * LANES:(h + 1) * LANES,
                    ]

    def cut_out(d, lo, hi):
        q, r = d // part, d % part
        return acc[q, pl.ds(lo * part + r, hi - lo, stride=part), :].astype(jnp.bfloat16)

    def send_owner(d, send_one):
        a, b = d // chan, d % chan
        xa, ka = b // cores, b % cores

        @pl.when((a != f) | (b != c))
        def _():
            send_one(
                ((a - f + fft) % fft, (xa - x + xs) % xs, (ka - core + cores) % cores)
            ).start()

    def upper(q):
        for d in range(q * part, (q + 1) * part):
            early[d] = cut_out(d, cut, blocks + MAXD)
            send_owner(d, send_early)

    def lower(q):
        for d in range(q * part, (q + 1) * part):
            late[d] = cut_out(d, 0, cut)
            send_owner(d, send_late)

    for i in range(len(SEGMENTS)):
        fetch(i).wait()
        add(i, 0, PARTS if i < TOGETHER else 1)
        if starts[i] == columns // 2:
            pl.semaphore_wait(barrier, len(partners))
            for q in range(PARTS if i < TOGETHER else 1):
                upper(q)
    lower(0)
    for q in range(1, PARTS):
        for i in range(TOGETHER, len(SEGMENTS)):
            add(i, q, q + 1)
            if starts[i] == columns // 2:
                upper(q)
        lower(q)
    for load in loads:
        load.start()

    loads[0].wait()
    loads[1].wait()
    accel = accel_ref[...]
    bank = bank_ref.shape[2]
    accels = accel.shape[1]
    taps = bank_ref.shape[1]
    chosen = jnp.where(
        lax.broadcasted_iota(jnp.int32, (bank, accels), 0) == accel, 1.0, 0.0
    ).astype(jnp.bfloat16)
    rows = []
    for part_index in range(2):
        row = dot(bank_ref[part_index], chosen)
        row = jnp.concatenate([row, jnp.zeros((LANES - taps, accels), jnp.float32)], axis=0)
        rows.append(row.T)
    for kk in range(LANES // 2):
        for part_index in range(2):
            shifted = pltpu.roll(rows[part_index], kk, 1) if kk else rows[part_index]
            tmat[kk * accels:(kk + 1) * accels, part_index * LANES:(part_index + 1) * LANES] = (
                shifted.astype(jnp.bfloat16)
            )
    for load in loads[2:]:
        load.wait()

    own = f * chan + c
    everything(early_in, early_in_sem).wait()
    everything(late_in, late_in_sem).wait()

    def gathered(z, own_ref, in_ref, lo, hi):
        base = ((f + fft - z) % fft) * chan
        total = None
        for k in range(chan):
            value = in_ref[base + k, lo:hi, :].astype(jnp.float32)
            total = value if total is None else total + value
        return total

    early_in[0] = early[own]
    late_in[0] = late[own]
    for z in range(fft):
        body = gathered(z, late, late_in, MAXD, cut)
        if z + 1 < fft:
            tail = gathered(z, early, early_in, 0, blocks + MAXD - cut)
            lead = gathered(z + 1, late, late_in, 0, MAXD)
            gap = tail.shape[0] - MAXD
            if gap:
                tail = jnp.concatenate([tail[:gap], tail[gap:] + lead], axis=0)
            else:
                tail = tail + lead
        else:
            tail = gathered(z, early, early_in, 0, blocks + MAXD - cut)
        grid_ref[z * blocks:z * blocks + cut - MAXD, :] = body
        grid_ref[z * blocks + cut - MAXD:(z + 1) * blocks, :] = tail

    wide = grid_ref.shape[0]
    half = wide // 2
    data = grid_ref[...] if wide == LANES else grid_ref[...].reshape(LANES, wide)
    high, low = split(data)
    both = jnp.concatenate(
        [
            jnp.concatenate([high, low], axis=1),
            jnp.concatenate([high, jnp.zeros_like(low)], axis=1),
        ],
        axis=0,
    )
    mixed = dot(one_ref[...], both)
    mixed = mixed[:, :wide] + mixed[:, wide:]
    re, im = mixed[:LANES], mixed[LANES:]
    tc, ts = twist_ref[0], twist_ref[1]
    turned = jnp.concatenate([re * tc + im * ts, im * tc - re * ts], axis=1)
    high, low = split(turned)
    spec = dot(high, two_ref[0]) + dot(low, two_ref[0]) + dot(high, two_ref[1])

    lane = lax.broadcasted_iota(jnp.int32, (16, 2 * half), 1)
    low64 = lax.broadcasted_iota(jnp.int32, (64, 2 * half), 1) < half
    low16 = lane < half
    sides = []
    square = jnp.zeros((LANES, 2 * half), jnp.float32)
    for part_index in range(2):
        o = spec[:, part_index * 2 * half:(part_index + 1) * 2 * half]
        square = square + o * o
        before = jnp.where(lane == 0, 0.0, pltpu.roll(o[LANES - 16:], 1, 1))
        after = jnp.where(lane == 2 * half - 1, 0.0, pltpu.roll(o[:16], 2 * half - 1, 1))
        sides.append(
            jnp.concatenate(
                [
                    jnp.where(low16, before, o[48:64]),
                    jnp.where(low64, o[:64], o[64:]),
                    jnp.where(low16, o[64:80], after),
                    jnp.zeros((32, 2 * half), jnp.float32),
                ],
                axis=0,
            ).astype(jnp.bfloat16)
        )
    energy_ref[0] = jnp.sum(square) * 0.5
    sr, si = sides
    window = jnp.concatenate(
        [jnp.concatenate([sr, si], axis=1), jnp.concatenate([-si, sr], axis=1)], axis=0
    )
    best = jnp.zeros((accels, 2 * half), jnp.float32)
    group = 8
    for g in range(LANES // 2 // group):
        out = dot(tmat[g * group * accels:(g + 1) * group * accels, :], window)
        for kk in range(group):
            rr = out[kk * accels:(kk + 1) * accels, :2 * half]
            ii = out[kk * accels:(kk + 1) * accels, 2 * half:]
            best = jnp.maximum(best, rr * rr + ii * ii)
    best = jnp.maximum(best, pltpu.roll(best, half, 1))
    peaks_ref[0] = best[:, :half]
    everything(early, early_out_sem).wait()
    everything(late, late_out_sem).wait()


def finish(found_ref, total_ref, peaks_ref, energy_ref):
    peaks_ref[...] = found_ref[...]
    energy_ref[0] = total_ref[0]


def solution(mesh):
    fft, chan = mesh.shape["fft"], mesh.shape["chan"]
    cores = 2
    xs = chan // cores

    def body(filterbank, delays, template_bank, accel_index):
        channels, samples = filterbank.shape
        dms = delays.shape[1]
        accels = accel_index.shape[0]
        length = samples * fft
        blocks = samples // LANES
        wide = length // LANES
        cut = blocks // 2 + MAXD
        rest = blocks + MAXD - cut
        one, twist, two = tables(length, channels * chan)
        bank = template_bank.transpose(0, 2, 1)
        accel = accel_index[None, :]
        f32, bf16 = jnp.float32, jnp.bfloat16
        dma = pltpu.SemaphoreType.DMA
        hbm = pl.BlockSpec(memory_space=pltpu.HBM)
        vmem = pl.BlockSpec(memory_space=pltpu.VMEM)

        def like(a):
            return pltpu.VMEM(a.shape, a.dtype)

        found, total = pl.pallas_call(
            functools.partial(kernel, (fft, xs, cores, dms, blocks)),
            out_shape=(
                pltpu.VMEM((1, accels, wide // 2), f32),
                pltpu.SMEM((1,), f32),
            ),
            in_specs=[hbm] * 7,
            out_specs=(vmem, pl.BlockSpec(memory_space=pltpu.SMEM)),
            scratch_shapes=[
                pltpu.VMEM((dms, channels), jnp.int32),
                pltpu.VMEM((channels, samples), bf16),
                pltpu.VMEM((MAXD * dms, channels), bf16),
                pltpu.VMEM((PARTS, (blocks + MAXD) * dms // PARTS, LANES), f32),
                pltpu.VMEM((dms, rest, LANES), bf16),
                pltpu.VMEM((dms, cut, LANES), bf16),
                pltpu.VMEM((dms, rest, LANES), bf16),
                pltpu.VMEM((dms, cut, LANES), bf16),
                pltpu.VMEM((wide, LANES), f32),
                like(bank), like(accel), like(one), like(twist), like(two),
                pltpu.VMEM((LANES // 2 * accels, 2 * LANES), bf16),
                dma, dma((len(SEGMENTS),)), dma((5,)), dma, dma, dma, dma,
            ],
            compiler_params=pltpu.CompilerParams(
                collective_id=0, has_side_effects=True, vmem_limit_bytes=56 * 2 ** 20
            ),
            name="search",
        )(filterbank, delays.T, bank, accel, one, twist, two)

        return pl.pallas_call(
            finish,
            out_shape=(
                jax.ShapeDtypeStruct(found.shape, f32),
                jax.ShapeDtypeStruct(total.shape, f32),
            ),
            in_specs=[vmem, pl.BlockSpec(memory_space=pltpu.SMEM)],
            out_specs=(vmem, pl.BlockSpec(memory_space=pltpu.SMEM)),
            name="finish",
        )(pltpu.with_memory_space_constraint(found, pltpu.VMEM), pltpu.with_memory_space_constraint(total, pltpu.SMEM))

    in_specs = (P(("beam", "chan"), "fft"), P("chan", None), P(), P())
    out_specs = (P(("beam", "fft", "chan"), None, None), P(("beam", "fft", "chan")))
    return jax.shard_map(body, mesh=mesh, in_specs=in_specs, out_specs=out_specs, check_vma=False)
```

```python
import functools

import jax
import jax.numpy as jnp
import ml_dtypes
import numpy as np
from jax import lax
from jax.experimental import pallas as pl
from jax.experimental.pallas import tpu as pltpu
from jax.sharding import PartitionSpec as P

MAXD = 16
LANES = 128
PARTS = 2
TOGETHER = 1
SEGMENTS = ((1, 0), (1, 1), (1, 1), (1, 1))
MESH = pl.DeviceIdType.MESH


def halves(table):
    high = table.astype(np.float32).astype(ml_dtypes.bfloat16)
    low = (table - high.astype(np.float64)).astype(np.float32).astype(ml_dtypes.bfloat16)
    return high, low


def tables(length, channels_total):
    wide = length // LANES
    half = wide // 2
    rows = np.arange(LANES)
    cols = np.arange(wide)
    outs = np.arange(half)
    first = 2 * np.pi * (rows[:, None] * rows[None, :] % LANES) / LANES
    one = np.concatenate([np.cos(first), -np.sin(first)], axis=0)
    turn = 2 * np.pi * (rows[:, None] * cols[None, :] % length) / length
    scale = channels_total ** -0.5 * length ** -0.5
    twist = np.stack([np.cos(turn), np.sin(turn)]) * scale
    second = 2 * np.pi * (cols[:, None] * outs[None, :] % wide) / wide
    c2, s2 = np.cos(second), np.sin(second)
    real = np.concatenate([c2, s2], axis=0)
    imag = np.concatenate([-s2, c2], axis=0)
    two = np.concatenate([real, real, imag, imag], axis=1)
    one = np.concatenate(halves(one), axis=1)
    two = np.stack(halves(two))
    return jnp.asarray(one), jnp.asarray(twist, jnp.float32), jnp.asarray(two)


def split(x):
    high = x.astype(jnp.bfloat16)
    return high, (x - high.astype(jnp.float32)).astype(jnp.bfloat16)


def dot(a, b):
    return jnp.dot(a, b, preferred_element_type=jnp.float32)


def kernel(
    sizes,
    fb_ref, delay_hbm, bank_hbm, accel_hbm, one_hbm, twist_hbm, two_hbm,
    peaks_ref, energy_ref,
    delay_ref, xbuf, picked, acc, early, late, early_in, late_in, grid_ref,
    bank_ref, accel_ref, one_ref, twist_ref, two_ref, tmat,
    lsem, fsem, tsem, early_out_sem, early_in_sem, late_out_sem, late_in_sem,
):
    fft, xs, cores, dms, blocks = sizes
    chan = xs * cores
    cut = blocks // 2 + MAXD
    f = lax.axis_index("fft")
    c = lax.axis_index("chan")
    x, core = c // cores, c % cores
    columns = fb_ref.shape[1]
    unit = columns // sum(n for n, _ in SEGMENTS)
    count = fft * chan
    part = dms // PARTS
    partners = [
        (g, s, k) for g in range(fft) for s in range(xs) for k in range(cores) if (g, s, k) != (0, 0, 0)
    ]
    far_first = sorted(partners, key=lambda p: (-min(p[0], fft - p[0]) - p[1], -p[2]))

    ends = [columns - unit * sum(n for n, _ in SEGMENTS[:i]) for i in range(len(SEGMENTS))]
    starts = ends[1:] + [0]

    def fetch(i):
        return pltpu.make_async_copy(
            fb_ref.at[:, starts[i]:ends[i]], xbuf.at[:, starts[i]:ends[i]], fsem.at[i]
        )

    loads = [
        pltpu.make_async_copy(a, b, tsem.at[i])
        for i, (a, b) in enumerate(
            [
                (bank_hbm, bank_ref), (accel_hbm, accel_ref), (one_hbm, one_ref),
                (twist_hbm, twist_ref), (two_hbm, two_ref),
            ]
        )
    ]
    lags = pltpu.make_async_copy(delay_hbm, delay_ref, lsem)
    lags.start()
    for i, (_, priority) in enumerate(SEGMENTS):
        fetch(i).start(priority=priority)

    def place(p):
        g, s, k = p
        return (f + g) % fft, ((x + s) % xs) * cores + (core + k) % cores

    barrier = pltpu.get_barrier_semaphore()
    for p in partners:
        g, d = place(p)
        pl.semaphore_signal(barrier, inc=1, device_id={"fft": g, "chan": d}, device_id_type=MESH)

    acc[...] = jnp.zeros_like(acc)
    lags.wait()
    lag = delay_ref[...]
    for q in range(PARTS):
        own_lag = lag[q * part:(q + 1) * part]
        for o in range(0, MAXD, 2):
            hits = [jnp.where(own_lag == o + 1 - n, 1.0, 0.0) for n in range(2)]
            row = (q * MAXD + MAXD - 2 - o) * part
            picked[row:row + 2 * part, :] = jnp.concatenate(hits, axis=0).astype(jnp.bfloat16)

    def slot(p):
        return (p[0] * xs + p[1]) * cores + p[2]

    def send(p, out, into, out_sem, in_sem):
        g, d = place(p)
        return pltpu.make_async_remote_copy(
            out.at[g * chan + d], into.at[slot(p)], out_sem, in_sem,
            device_id={"fft": g, "chan": d}, device_id_type=MESH,
        )

    def send_early(p):
        return send(p, early, early_in, early_out_sem, early_in_sem)

    def send_late(p):
        return send(p, late, late_in, late_out_sem, late_in_sem)

    def everything(ref, sem):
        slots = ref.at[pl.ds(1, count - 1)]
        return pltpu.make_async_copy(slots, slots, sem)

    def add(i, first, last):
        for b in range(starts[i] // 256, ends[i] // 256):
            y = dot(
                picked[first * MAXD * part:last * MAXD * part, :], xbuf[:, b * 256:(b + 1) * 256]
            )
            for q in range(first, last):
                for h in range(2):
                    row = (2 * b + h + 1) * part
                    acc[q, row:row + MAXD * part, :] += y[
                        (q - first) * MAXD * part:(q - first + 1) * MAXD * part,
                        h * LANES:(h + 1) * LANES,
                    ]

    def cut_out(d, lo, hi):
        q, r = d // part, d % part
        return acc[q, pl.ds(lo * part + r, hi - lo, stride=part), :].astype(jnp.bfloat16)

    def send_owner(d, send_one):
        a, b = d // chan, d % chan
        xa, ka = b // cores, b % cores

        @pl.when((a != f) | (b != c))
        def _():
            send_one(
                ((a - f + fft) % fft, (xa - x + xs) % xs, (ka - core + cores) % cores)
            ).start()

    def upper(q):
        for d in range(q * part, (q + 1) * part):
            early[d] = cut_out(d, cut, blocks + MAXD)
            send_owner(d, send_early)

    def lower(q):
        for d in range(q * part, (q + 1) * part):
            late[d] = cut_out(d, 0, cut)
            send_owner(d, send_late)

    for i in range(len(SEGMENTS)):
        fetch(i).wait()
        add(i, 0, PARTS if i < TOGETHER else 1)
        if starts[i] == columns // 2:
            pl.semaphore_wait(barrier, len(partners))
            for q in range(PARTS if i < TOGETHER else 1):
                upper(q)
    lower(0)
    for q in range(1, PARTS):
        for i in range(TOGETHER, len(SEGMENTS)):
            add(i, q, q + 1)
            if starts[i] == columns // 2:
                upper(q)
        lower(q)
    for load in loads:
        load.start()

    loads[0].wait()
    loads[1].wait()
    accel = accel_ref[...]
    bank = bank_ref.shape[2]
    accels = accel.shape[1]
    taps = bank_ref.shape[1]
    chosen = jnp.where(
        lax.broadcasted_iota(jnp.int32, (bank, accels), 0) == accel, 1.0, 0.0
    ).astype(jnp.bfloat16)
    rows = []
    for part_index in range(2):
        row = dot(bank_ref[part_index], chosen)
        row = jnp.concatenate([row, jnp.zeros((LANES - taps, accels), jnp.float32)], axis=0)
        rows.append(row.T)
    for kk in range(LANES // 2):
        for part_index in range(2):
            shifted = pltpu.roll(rows[part_index], kk, 1) if kk else rows[part_index]
            tmat[kk * accels:(kk + 1) * accels, part_index * LANES:(part_index + 1) * LANES] = (
                shifted.astype(jnp.bfloat16)
            )
    for load in loads[2:]:
        load.wait()

    own = f * chan + c
    everything(early_in, early_in_sem).wait()
    everything(late_in, late_in_sem).wait()

    def gathered(z, own_ref, in_ref, lo, hi):
        base = ((f + fft - z) % fft) * chan
        total = None
        for k in range(chan):
            value = in_ref[base + k, lo:hi, :].astype(jnp.float32)
            total = value if total is None else total + value
        return total

    early_in[0] = early[own]
    late_in[0] = late[own]
    for z in range(fft):
        body = gathered(z, late, late_in, MAXD, cut)
        if z + 1 < fft:
            tail = gathered(z, early, early_in, 0, blocks + MAXD - cut)
            lead = gathered(z + 1, late, late_in, 0, MAXD)
            gap = tail.shape[0] - MAXD
            if gap:
                tail = jnp.concatenate([tail[:gap], tail[gap:] + lead], axis=0)
            else:
                tail = tail + lead
        else:
            tail = gathered(z, early, early_in, 0, blocks + MAXD - cut)
        grid_ref[z * blocks:z * blocks + cut - MAXD, :] = body
        grid_ref[z * blocks + cut - MAXD:(z + 1) * blocks, :] = tail

    wide = grid_ref.shape[0]
    half = wide // 2
    data = grid_ref[...] if wide == LANES else grid_ref[...].reshape(LANES, wide)
    high, low = split(data)
    both = jnp.concatenate(
        [
            jnp.concatenate([high, low], axis=1),
            jnp.concatenate([high, jnp.zeros_like(low)], axis=1),
        ],
        axis=0,
    )
    mixed = dot(one_ref[...], both)
    mixed = mixed[:, :wide] + mixed[:, wide:]
    re, im = mixed[:LANES], mixed[LANES:]
    tc, ts = twist_ref[0], twist_ref[1]
    turned = jnp.concatenate([re * tc + im * ts, im * tc - re * ts], axis=1)
    high, low = split(turned)
    pair = dot(jnp.concatenate([high, low], axis=0), two_ref[0])
    spec = pair[:LANES] + pair[LANES:] + dot(high, two_ref[1])

    lane = lax.broadcasted_iota(jnp.int32, (16, 2 * half), 1)
    low64 = lax.broadcasted_iota(jnp.int32, (64, 2 * half), 1) < half
    low16 = lane < half
    sides = []
    square = jnp.zeros((LANES, 2 * half), jnp.float32)
    for part_index in range(2):
        o = spec[:, part_index * 2 * half:(part_index + 1) * 2 * half]
        square = square + o * o
        before = jnp.where(lane == 0, 0.0, pltpu.roll(o[LANES - 16:], 1, 1))
        after = jnp.where(lane == 2 * half - 1, 0.0, pltpu.roll(o[:16], 2 * half - 1, 1))
        sides.append(
            jnp.concatenate(
                [
                    jnp.where(low16, before, o[48:64]),
                    jnp.where(low64, o[:64], o[64:]),
                    jnp.where(low16, o[64:80], after),
                    jnp.zeros((32, 2 * half), jnp.float32),
                ],
                axis=0,
            ).astype(jnp.bfloat16)
        )
    energy_ref[0] = jnp.sum(square) * 0.5
    sr, si = sides
    window = jnp.concatenate(
        [jnp.concatenate([sr, si], axis=1), jnp.concatenate([-si, sr], axis=1)], axis=0
    )
    best = jnp.zeros((accels, 2 * half), jnp.float32)
    group = 8
    for g in range(LANES // 2 // group):
        out = dot(tmat[g * group * accels:(g + 1) * group * accels, :], window)
        for kk in range(group):
            rr = out[kk * accels:(kk + 1) * accels, :2 * half]
            ii = out[kk * accels:(kk + 1) * accels, 2 * half:]
            best = jnp.maximum(best, rr * rr + ii * ii)
    best = jnp.maximum(best, pltpu.roll(best, half, 1))
    peaks_ref[0] = best[:, :half]
    everything(early, early_out_sem).wait()
    everything(late, late_out_sem).wait()


def finish(found_ref, total_ref, peaks_ref, energy_ref):
    peaks_ref[...] = found_ref[...]
    energy_ref[0] = total_ref[0]


def solution(mesh):
    fft, chan = mesh.shape["fft"], mesh.shape["chan"]
    cores = 2
    xs = chan // cores

    def body(filterbank, delays, template_bank, accel_index):
        channels, samples = filterbank.shape
        dms = delays.shape[1]
        accels = accel_index.shape[0]
        length = samples * fft
        blocks = samples // LANES
        wide = length // LANES
        cut = blocks // 2 + MAXD
        rest = blocks + MAXD - cut
        one, twist, two = tables(length, channels * chan)
        bank = template_bank.transpose(0, 2, 1)
        accel = accel_index[None, :]
        f32, bf16 = jnp.float32, jnp.bfloat16
        dma = pltpu.SemaphoreType.DMA
        hbm = pl.BlockSpec(memory_space=pltpu.HBM)
        vmem = pl.BlockSpec(memory_space=pltpu.VMEM)

        def like(a):
            return pltpu.VMEM(a.shape, a.dtype)

        found, total = pl.pallas_call(
            functools.partial(kernel, (fft, xs, cores, dms, blocks)),
            out_shape=(
                pltpu.VMEM((1, accels, wide // 2), f32),
                pltpu.SMEM((1,), f32),
            ),
            in_specs=[hbm] * 7,
            out_specs=(vmem, pl.BlockSpec(memory_space=pltpu.SMEM)),
            scratch_shapes=[
                pltpu.VMEM((dms, channels), jnp.int32),
                pltpu.VMEM((channels, samples), bf16),
                pltpu.VMEM((MAXD * dms, channels), bf16),
                pltpu.VMEM((PARTS, (blocks + MAXD) * dms // PARTS, LANES), f32),
                pltpu.VMEM((dms, rest, LANES), bf16),
                pltpu.VMEM((dms, cut, LANES), bf16),
                pltpu.VMEM((dms, rest, LANES), bf16),
                pltpu.VMEM((dms, cut, LANES), bf16),
                pltpu.VMEM((wide, LANES), f32),
                like(bank), like(accel), like(one), like(twist), like(two),
                pltpu.VMEM((LANES // 2 * accels, 2 * LANES), bf16),
                dma, dma((len(SEGMENTS),)), dma((5,)), dma, dma, dma, dma,
            ],
            compiler_params=pltpu.CompilerParams(
                collective_id=0, has_side_effects=True, vmem_limit_bytes=56 * 2 ** 20
            ),
            name="search",
        )(filterbank, delays.T, bank, accel, one, twist, two)

        return pl.pallas_call(
            finish,
            out_shape=(
                jax.ShapeDtypeStruct(found.shape, f32),
                jax.ShapeDtypeStruct(total.shape, f32),
            ),
            in_specs=[vmem, pl.BlockSpec(memory_space=pltpu.SMEM)],
            out_specs=(vmem, pl.BlockSpec(memory_space=pltpu.SMEM)),
            name="finish",
        )(pltpu.with_memory_space_constraint(found, pltpu.VMEM), pltpu.with_memory_space_constraint(total, pltpu.SMEM))

    in_specs = (P(("beam", "chan"), "fft"), P("chan", None), P(), P())
    out_specs = (P(("beam", "fft", "chan"), None, None), P(("beam", "fft", "chan")))
    return jax.shard_map(body, mesh=mesh, in_specs=in_specs, out_specs=out_specs, check_vma=False)
```

```python
import functools

import jax
import jax.numpy as jnp
import ml_dtypes
import numpy as np
from jax import lax
from jax.experimental import pallas as pl
from jax.experimental.pallas import tpu as pltpu
from jax.sharding import PartitionSpec as P

MAXD = 16
LANES = 128
PARTS = 2
TOGETHER = 1
SEGMENTS = ((1, 0), (1, 1), (1, 1), (1, 1))
MESH = pl.DeviceIdType.MESH


def halves(table):
    high = table.astype(np.float32).astype(ml_dtypes.bfloat16)
    low = (table - high.astype(np.float64)).astype(np.float32).astype(ml_dtypes.bfloat16)
    return high, low


def tables(length, channels_total):
    wide = length // LANES
    half = wide // 2
    rows = np.arange(LANES)
    cols = np.arange(wide)
    outs = np.arange(half)
    first = 2 * np.pi * (rows[:, None] * rows[None, :] % LANES) / LANES
    one = np.concatenate([np.cos(first), -np.sin(first)], axis=0)
    turn = 2 * np.pi * (rows[:, None] * cols[None, :] % length) / length
    scale = channels_total ** -0.5 * length ** -0.5
    twist = np.stack([np.cos(turn), np.sin(turn)]) * scale
    second = 2 * np.pi * (cols[:, None] * outs[None, :] % wide) / wide
    c2, s2 = np.cos(second), np.sin(second)
    real = np.concatenate([c2, s2], axis=0)
    imag = np.concatenate([-s2, c2], axis=0)
    two = np.concatenate([real, real, imag, imag], axis=1)
    one = np.concatenate(halves(one), axis=1)
    two = np.stack(halves(two))
    return jnp.asarray(one), jnp.asarray(twist, jnp.float32), jnp.asarray(two)


def split(x):
    high = x.astype(jnp.bfloat16)
    return high, (x - high.astype(jnp.float32)).astype(jnp.bfloat16)


def dot(a, b):
    return jnp.dot(a, b, preferred_element_type=jnp.float32)


def kernel(
    sizes,
    fb_ref, delay_hbm, bank_hbm, accel_hbm, one_hbm, twist_hbm, two_hbm,
    peaks_ref, energy_ref,
    delay_ref, xbuf, picked, acc, early, late, early_in, late_in, grid_ref,
    bank_ref, accel_ref, one_ref, twist_ref, two_ref, tmat,
    lsem, fsem, tsem, early_out_sem, early_in_sem, late_out_sem, late_in_sem,
):
    fft, xs, cores, dms, blocks = sizes
    chan = xs * cores
    cut = blocks // 2 + MAXD
    f = lax.axis_index("fft")
    c = lax.axis_index("chan")
    x, core = c // cores, c % cores
    columns = fb_ref.shape[1]
    unit = columns // sum(n for n, _ in SEGMENTS)
    count = fft * chan
    part = dms // PARTS
    partners = [
        (g, s, k) for g in range(fft) for s in range(xs) for k in range(cores) if (g, s, k) != (0, 0, 0)
    ]
    far_first = sorted(partners, key=lambda p: (-min(p[0], fft - p[0]) - p[1], -p[2]))

    ends = [columns - unit * sum(n for n, _ in SEGMENTS[:i]) for i in range(len(SEGMENTS))]
    starts = ends[1:] + [0]

    def fetch(i):
        return pltpu.make_async_copy(
            fb_ref.at[:, starts[i]:ends[i]], xbuf.at[:, starts[i]:ends[i]], fsem.at[i]
        )

    loads = [
        pltpu.make_async_copy(a, b, tsem.at[i])
        for i, (a, b) in enumerate(
            [
                (bank_hbm, bank_ref), (accel_hbm, accel_ref), (one_hbm, one_ref),
                (twist_hbm, twist_ref), (two_hbm, two_ref),
            ]
        )
    ]
    lags = pltpu.make_async_copy(delay_hbm, delay_ref, lsem)
    lags.start()
    for i, (_, priority) in enumerate(SEGMENTS):
        fetch(i).start(priority=priority)

    def place(p):
        g, s, k = p
        return (f + g) % fft, ((x + s) % xs) * cores + (core + k) % cores

    barrier = pltpu.get_barrier_semaphore()
    for p in partners:
        g, d = place(p)
        pl.semaphore_signal(barrier, inc=1, device_id={"fft": g, "chan": d}, device_id_type=MESH)

    acc[...] = jnp.zeros_like(acc)
    lags.wait()
    lag = delay_ref[...]
    for q in range(PARTS):
        own_lag = lag[q * part:(q + 1) * part]
        for o in range(0, MAXD, 2):
            hits = [jnp.where(own_lag == o + 1 - n, 1.0, 0.0) for n in range(2)]
            row = (q * MAXD + MAXD - 2 - o) * part
            picked[row:row + 2 * part, :] = jnp.concatenate(hits, axis=0).astype(jnp.bfloat16)

    def slot(p):
        return (p[0] * xs + p[1]) * cores + p[2]

    def send(p, out, into, out_sem, in_sem):
        g, d = place(p)
        return pltpu.make_async_remote_copy(
            out.at[g * chan + d], into.at[slot(p)], out_sem, in_sem,
            device_id={"fft": g, "chan": d}, device_id_type=MESH,
        )

    def send_early(p):
        return send(p, early, early_in, early_out_sem, early_in_sem)

    def send_late(p):
        return send(p, late, late_in, late_out_sem, late_in_sem)

    def everything(ref, sem):
        slots = ref.at[pl.ds(1, count - 1)]
        return pltpu.make_async_copy(slots, slots, sem)

    def add(i, first, last):
        for b in range(starts[i] // 256, ends[i] // 256):
            y = dot(
                picked[first * MAXD * part:last * MAXD * part, :], xbuf[:, b * 256:(b + 1) * 256]
            )
            for q in range(first, last):
                for h in range(2):
                    row = (2 * b + h + 1) * part
                    acc[q, row:row + MAXD * part, :] += y[
                        (q - first) * MAXD * part:(q - first + 1) * MAXD * part,
                        h * LANES:(h + 1) * LANES,
                    ]

    def cut_out(d, lo, hi):
        q, r = d // part, d % part
        return acc[q, pl.ds(lo * part + r, hi - lo, stride=part), :].astype(jnp.bfloat16)

    def send_owner(d, send_one):
        a, b = d // chan, d % chan
        xa, ka = b // cores, b % cores

        @pl.when(f * chan + c != d)
        def _():
            send_one(
                ((a - f + fft) % fft, (xa - x + xs) % xs, (ka - core + cores) % cores)
            ).start()

    def upper(q):
        for d in range(q * part, (q + 1) * part):
            early[d] = cut_out(d, cut, blocks + MAXD)
        for d in range(q * part, (q + 1) * part):
            send_owner(d, send_early)

    def lower(q):
        for d in range(q * part, (q + 1) * part):
            late[d] = cut_out(d, 0, cut)
        for d in range(q * part, (q + 1) * part):
            send_owner(d, send_late)

    for i in range(len(SEGMENTS)):
        fetch(i).wait()
        add(i, 0, PARTS if i < TOGETHER else 1)
        if starts[i] == columns // 2:
            pl.semaphore_wait(barrier, len(partners))
            for q in range(PARTS if i < TOGETHER else 1):
                upper(q)
    lower(0)
    for q in range(1, PARTS):
        for i in range(TOGETHER, len(SEGMENTS)):
            add(i, q, q + 1)
            if starts[i] == columns // 2:
                upper(q)
        lower(q)
    for load in loads:
        load.start()

    loads[0].wait()
    loads[1].wait()
    accel = accel_ref[...]
    bank = bank_ref.shape[2]
    accels = accel.shape[1]
    taps = bank_ref.shape[1]
    chosen = jnp.where(
        lax.broadcasted_iota(jnp.int32, (bank, accels), 0) == accel, 1.0, 0.0
    ).astype(jnp.bfloat16)
    rows = []
    for part_index in range(2):
        row = dot(bank_ref[part_index], chosen)
        row = jnp.concatenate([row, jnp.zeros((LANES - taps, accels), jnp.float32)], axis=0)
        rows.append(row.T)
    for kk in range(LANES // 2):
        for part_index in range(2):
            shifted = pltpu.roll(rows[part_index], kk, 1) if kk else rows[part_index]
            tmat[kk * accels:(kk + 1) * accels, part_index * LANES:(part_index + 1) * LANES] = (
                shifted.astype(jnp.bfloat16)
            )
    for load in loads[2:]:
        load.wait()

    own = f * chan + c
    everything(early_in, early_in_sem).wait()
    everything(late_in, late_in_sem).wait()

    def gathered(z, own_ref, in_ref, lo, hi):
        base = ((f + fft - z) % fft) * chan
        total = None
        for k in range(chan):
            value = in_ref[base + k, lo:hi, :].astype(jnp.float32)
            total = value if total is None else total + value
        return total

    early_in[0] = early[own]
    late_in[0] = late[own]
    for z in range(fft):
        body = gathered(z, late, late_in, MAXD, cut)
        if z + 1 < fft:
            tail = gathered(z, early, early_in, 0, blocks + MAXD - cut)
            lead = gathered(z + 1, late, late_in, 0, MAXD)
            gap = tail.shape[0] - MAXD
            if gap:
                tail = jnp.concatenate([tail[:gap], tail[gap:] + lead], axis=0)
            else:
                tail = tail + lead
        else:
            tail = gathered(z, early, early_in, 0, blocks + MAXD - cut)
        grid_ref[z * blocks:z * blocks + cut - MAXD, :] = body
        grid_ref[z * blocks + cut - MAXD:(z + 1) * blocks, :] = tail

    wide = grid_ref.shape[0]
    half = wide // 2
    data = grid_ref[...] if wide == LANES else grid_ref[...].reshape(LANES, wide)
    high, low = split(data)
    both = jnp.concatenate(
        [
            jnp.concatenate([high, low], axis=1),
            jnp.concatenate([high, jnp.zeros_like(low)], axis=1),
        ],
        axis=0,
    )
    mixed = dot(one_ref[...], both)
    mixed = mixed[:, :wide] + mixed[:, wide:]
    re, im = mixed[:LANES], mixed[LANES:]
    tc, ts = twist_ref[0], twist_ref[1]
    turned = jnp.concatenate([re * tc + im * ts, im * tc - re * ts], axis=1)
    high, low = split(turned)
    pair = dot(jnp.concatenate([high, low], axis=0), two_ref[0])
    spec = pair[:LANES] + pair[LANES:] + dot(high, two_ref[1])

    lane = lax.broadcasted_iota(jnp.int32, (16, 2 * half), 1)
    low64 = lax.broadcasted_iota(jnp.int32, (64, 2 * half), 1) < half
    low16 = lane < half
    sides = []
    square = jnp.zeros((LANES, 2 * half), jnp.float32)
    for part_index in range(2):
        o = spec[:, part_index * 2 * half:(part_index + 1) * 2 * half]
        square = square + o * o
        before = jnp.where(lane == 0, 0.0, pltpu.roll(o[LANES - 16:], 1, 1))
        after = jnp.where(lane == 2 * half - 1, 0.0, pltpu.roll(o[:16], 2 * half - 1, 1))
        sides.append(
            jnp.concatenate(
                [
                    jnp.where(low16, before, o[48:64]),
                    jnp.where(low64, o[:64], o[64:]),
                    jnp.where(low16, o[64:80], after),
                    jnp.zeros((32, 2 * half), jnp.float32),
                ],
                axis=0,
            ).astype(jnp.bfloat16)
        )
    energy_ref[0] = jnp.sum(square) * 0.5
    sr, si = sides
    window = jnp.concatenate(
        [jnp.concatenate([sr, si], axis=1), jnp.concatenate([-si, sr], axis=1)], axis=0
    )
    best = jnp.zeros((accels, 2 * half), jnp.float32)
    group = 8
    for g in range(LANES // 2 // group):
        out = dot(tmat[g * group * accels:(g + 1) * group * accels, :], window)
        for kk in range(group):
            rr = out[kk * accels:(kk + 1) * accels, :2 * half]
            ii = out[kk * accels:(kk + 1) * accels, 2 * half:]
            best = jnp.maximum(best, rr * rr + ii * ii)
    best = jnp.maximum(best, pltpu.roll(best, half, 1))
    peaks_ref[0] = best[:, :half]
    everything(early, early_out_sem).wait()
    everything(late, late_out_sem).wait()


def finish(found_ref, total_ref, peaks_ref, energy_ref):
    peaks_ref[...] = found_ref[...]
    energy_ref[0] = total_ref[0]


def solution(mesh):
    fft, chan = mesh.shape["fft"], mesh.shape["chan"]
    cores = 2
    xs = chan // cores

    def body(filterbank, delays, template_bank, accel_index):
        channels, samples = filterbank.shape
        dms = delays.shape[1]
        accels = accel_index.shape[0]
        length = samples * fft
        blocks = samples // LANES
        wide = length // LANES
        cut = blocks // 2 + MAXD
        rest = blocks + MAXD - cut
        one, twist, two = tables(length, channels * chan)
        bank = template_bank.transpose(0, 2, 1)
        accel = accel_index[None, :]
        f32, bf16 = jnp.float32, jnp.bfloat16
        dma = pltpu.SemaphoreType.DMA
        hbm = pl.BlockSpec(memory_space=pltpu.HBM)
        vmem = pl.BlockSpec(memory_space=pltpu.VMEM)

        def like(a):
            return pltpu.VMEM(a.shape, a.dtype)

        found, total = pl.pallas_call(
            functools.partial(kernel, (fft, xs, cores, dms, blocks)),
            out_shape=(
                pltpu.VMEM((1, accels, wide // 2), f32),
                pltpu.SMEM((1,), f32),
            ),
            in_specs=[hbm] * 7,
            out_specs=(vmem, pl.BlockSpec(memory_space=pltpu.SMEM)),
            scratch_shapes=[
                pltpu.VMEM((dms, channels), jnp.int32),
                pltpu.VMEM((channels, samples), bf16),
                pltpu.VMEM((MAXD * dms, channels), bf16),
                pltpu.VMEM((PARTS, (blocks + MAXD) * dms // PARTS, LANES), f32),
                pltpu.VMEM((dms, rest, LANES), bf16),
                pltpu.VMEM((dms, cut, LANES), bf16),
                pltpu.VMEM((dms, rest, LANES), bf16),
                pltpu.VMEM((dms, cut, LANES), bf16),
                pltpu.VMEM((wide, LANES), f32),
                like(bank), like(accel), like(one), like(twist), like(two),
                pltpu.VMEM((LANES // 2 * accels, 2 * LANES), bf16),
                dma, dma((len(SEGMENTS),)), dma((5,)), dma, dma, dma, dma,
            ],
            compiler_params=pltpu.CompilerParams(
                collective_id=0, has_side_effects=True, vmem_limit_bytes=56 * 2 ** 20
            ),
            name="search",
        )(filterbank, delays.T, bank, accel, one, twist, two)

        return pl.pallas_call(
            finish,
            out_shape=(
                jax.ShapeDtypeStruct(found.shape, f32),
                jax.ShapeDtypeStruct(total.shape, f32),
            ),
            in_specs=[vmem, pl.BlockSpec(memory_space=pltpu.SMEM)],
            out_specs=(vmem, pl.BlockSpec(memory_space=pltpu.SMEM)),
            name="finish",
        )(pltpu.with_memory_space_constraint(found, pltpu.VMEM), pltpu.with_memory_space_constraint(total, pltpu.SMEM))

    in_specs = (P(("beam", "chan"), "fft"), P("chan", None), P(), P())
    out_specs = (P(("beam", "fft", "chan"), None, None), P(("beam", "fft", "chan")))
    return jax.shard_map(body, mesh=mesh, in_specs=in_specs, out_specs=out_specs, check_vma=False)
```

```python
import functools

import jax
import jax.numpy as jnp
import ml_dtypes
import numpy as np
from jax import lax
from jax.experimental import pallas as pl
from jax.experimental.pallas import tpu as pltpu
from jax.sharding import PartitionSpec as P

MAXD = 16
LANES = 128
PARTS = 2
TOGETHER = 1
SEGMENTS = ((1, 0), (1, 1), (1, 1), (1, 1))
MESH = pl.DeviceIdType.MESH


def halves(table):
    high = table.astype(np.float32).astype(ml_dtypes.bfloat16)
    low = (table - high.astype(np.float64)).astype(np.float32).astype(ml_dtypes.bfloat16)
    return high, low


def tables(length, channels_total):
    wide = length // LANES
    half = wide // 2
    rows = np.arange(LANES)
    cols = np.arange(wide)
    outs = np.arange(half)
    first = 2 * np.pi * (rows[:, None] * rows[None, :] % LANES) / LANES
    one = np.concatenate([np.cos(first), -np.sin(first)], axis=0)
    turn = 2 * np.pi * (rows[:, None] * cols[None, :] % length) / length
    scale = channels_total ** -0.5 * length ** -0.5
    twist = np.stack([np.cos(turn), np.sin(turn)]) * scale
    second = 2 * np.pi * (cols[:, None] * outs[None, :] % wide) / wide
    c2, s2 = np.cos(second), np.sin(second)
    real = np.concatenate([c2, s2], axis=0)
    imag = np.concatenate([-s2, c2], axis=0)
    two = np.concatenate([real, real, imag, imag], axis=1)
    one = np.concatenate(halves(one), axis=1)
    two = np.stack(halves(two))
    return jnp.asarray(one), jnp.asarray(twist, jnp.float32), jnp.asarray(two)


def split(x):
    high = x.astype(jnp.bfloat16)
    return high, (x - high.astype(jnp.float32)).astype(jnp.bfloat16)


def dot(a, b):
    return jnp.dot(a, b, preferred_element_type=jnp.float32)


def kernel(
    sizes,
    fb_ref, delay_hbm, bank_hbm, accel_hbm, one_hbm, twist_hbm, two_hbm,
    peaks_ref, energy_ref,
    delay_ref, xbuf, picked, acc, early, late, early_in, late_in, grid_ref,
    bank_ref, accel_ref, one_ref, twist_ref, two_ref, tmat,
    lsem, fsem, tsem, early_out_sem, early_in_sem, late_out_sem, late_in_sem,
):
    fft, xs, cores, dms, blocks = sizes
    chan = xs * cores
    cut = blocks // 2 + MAXD
    f = lax.axis_index("fft")
    c = lax.axis_index("chan")
    x, core = c // cores, c % cores
    columns = fb_ref.shape[1]
    unit = columns // sum(n for n, _ in SEGMENTS)
    count = fft * chan
    part = dms // PARTS
    partners = [
        (g, s, k) for g in range(fft) for s in range(xs) for k in range(cores) if (g, s, k) != (0, 0, 0)
    ]
    far_first = sorted(partners, key=lambda p: (-min(p[0], fft - p[0]) - p[1], -p[2]))

    ends = [columns - unit * sum(n for n, _ in SEGMENTS[:i]) for i in range(len(SEGMENTS))]
    starts = ends[1:] + [0]

    def fetch(i):
        return pltpu.make_async_copy(
            fb_ref.at[:, starts[i]:ends[i]], xbuf.at[:, starts[i]:ends[i]], fsem.at[i]
        )

    loads = [
        pltpu.make_async_copy(a, b, tsem.at[i])
        for i, (a, b) in enumerate(
            [
                (bank_hbm, bank_ref), (accel_hbm, accel_ref), (one_hbm, one_ref),
                (twist_hbm, twist_ref), (two_hbm, two_ref),
            ]
        )
    ]
    lags = pltpu.make_async_copy(delay_hbm, delay_ref, lsem)
    lags.start()
    fetch(0).start(priority=SEGMENTS[0][1])

    def place(p):
        g, s, k = p
        return (f + g) % fft, ((x + s) % xs) * cores + (core + k) % cores

    barrier = pltpu.get_barrier_semaphore()
    for p in partners:
        g, d = place(p)
        pl.semaphore_signal(barrier, inc=1, device_id={"fft": g, "chan": d}, device_id_type=MESH)
    for i, (_, priority) in enumerate(SEGMENTS[1:], 1):
        fetch(i).start(priority=priority)

    acc[...] = jnp.zeros_like(acc)
    lags.wait()
    lag = delay_ref[...]
    for q in range(PARTS):
        own_lag = lag[q * part:(q + 1) * part]
        for o in range(0, MAXD, 2):
            hits = [jnp.where(own_lag == o + 1 - n, 1.0, 0.0) for n in range(2)]
            row = (q * MAXD + MAXD - 2 - o) * part
            picked[row:row + 2 * part, :] = jnp.concatenate(hits, axis=0).astype(jnp.bfloat16)

    def slot(p):
        return (p[0] * xs + p[1]) * cores + p[2]

    def send(p, out, into, out_sem, in_sem):
        g, d = place(p)
        return pltpu.make_async_remote_copy(
            out.at[g * chan + d], into.at[slot(p)], out_sem, in_sem,
            device_id={"fft": g, "chan": d}, device_id_type=MESH,
        )

    def send_early(p):
        return send(p, early, early_in, early_out_sem, early_in_sem)

    def send_late(p):
        return send(p, late, late_in, late_out_sem, late_in_sem)

    def everything(ref, sem):
        slots = ref.at[pl.ds(1, count - 1)]
        return pltpu.make_async_copy(slots, slots, sem)

    def add(i, first, last):
        for b in range(starts[i] // 256, ends[i] // 256):
            y = dot(
                picked[first * MAXD * part:last * MAXD * part, :], xbuf[:, b * 256:(b + 1) * 256]
            )
            for q in range(first, last):
                for h in range(2):
                    row = (2 * b + h + 1) * part
                    acc[q, row:row + MAXD * part, :] += y[
                        (q - first) * MAXD * part:(q - first + 1) * MAXD * part,
                        h * LANES:(h + 1) * LANES,
                    ]

    def cut_out(d, lo, hi):
        q, r = d // part, d % part
        return acc[q, pl.ds(lo * part + r, hi - lo, stride=part), :].astype(jnp.bfloat16)

    def send_owner(d, send_one):
        a, b = d // chan, d % chan
        xa, ka = b // cores, b % cores

        @pl.when((a != f) | (b != c))
        def _():
            send_one(
                ((a - f + fft) % fft, (xa - x + xs) % xs, (ka - core + cores) % cores)
            ).start()

    def upper(q):
        for d in range(q * part, (q + 1) * part):
            early[d] = cut_out(d, cut, blocks + MAXD)
            send_owner(d, send_early)

    def lower(q):
        for d in range(q * part, (q + 1) * part):
            late[d] = cut_out(d, 0, cut)
            send_owner(d, send_late)

    for i in range(len(SEGMENTS)):
        fetch(i).wait()
        add(i, 0, PARTS if i < TOGETHER else 1)
        if starts[i] == columns // 2:
            pl.semaphore_wait(barrier, len(partners))
            for q in range(PARTS if i < TOGETHER else 1):
                upper(q)
    lower(0)
    for q in range(1, PARTS):
        for i in range(TOGETHER, len(SEGMENTS)):
            add(i, q, q + 1)
            if starts[i] == columns // 2:
                upper(q)
        lower(q)
    for load in loads:
        load.start()

    loads[0].wait()
    loads[1].wait()
    accel = accel_ref[...]
    bank = bank_ref.shape[2]
    accels = accel.shape[1]
    taps = bank_ref.shape[1]
    chosen = jnp.where(
        lax.broadcasted_iota(jnp.int32, (bank, accels), 0) == accel, 1.0, 0.0
    ).astype(jnp.bfloat16)
    rows = []
    for part_index in range(2):
        row = dot(bank_ref[part_index], chosen)
        row = jnp.concatenate([row, jnp.zeros((LANES - taps, accels), jnp.float32)], axis=0)
        rows.append(row.T)
    for kk in range(LANES // 2):
        for part_index in range(2):
            shifted = pltpu.roll(rows[part_index], kk, 1) if kk else rows[part_index]
            tmat[kk * accels:(kk + 1) * accels, part_index * LANES:(part_index + 1) * LANES] = (
                shifted.astype(jnp.bfloat16)
            )
    for load in loads[2:]:
        load.wait()

    own = f * chan + c
    everything(early_in, early_in_sem).wait()
    everything(late_in, late_in_sem).wait()

    def gathered(z, own_ref, in_ref, lo, hi):
        base = ((f + fft - z) % fft) * chan
        total = None
        for k in range(chan):
            value = in_ref[base + k, lo:hi, :].astype(jnp.float32)
            total = value if total is None else total + value
        return total

    early_in[0] = early[own]
    late_in[0] = late[own]
    for z in range(fft):
        body = gathered(z, late, late_in, MAXD, cut)
        if z + 1 < fft:
            tail = gathered(z, early, early_in, 0, blocks + MAXD - cut)
            lead = gathered(z + 1, late, late_in, 0, MAXD)
            gap = tail.shape[0] - MAXD
            if gap:
                tail = jnp.concatenate([tail[:gap], tail[gap:] + lead], axis=0)
            else:
                tail = tail + lead
        else:
            tail = gathered(z, early, early_in, 0, blocks + MAXD - cut)
        grid_ref[z * blocks:z * blocks + cut - MAXD, :] = body
        grid_ref[z * blocks + cut - MAXD:(z + 1) * blocks, :] = tail

    wide = grid_ref.shape[0]
    half = wide // 2
    data = grid_ref[...] if wide == LANES else grid_ref[...].reshape(LANES, wide)
    high, low = split(data)
    both = jnp.concatenate(
        [
            jnp.concatenate([high, low], axis=1),
            jnp.concatenate([high, jnp.zeros_like(low)], axis=1),
        ],
        axis=0,
    )
    mixed = dot(one_ref[...], both)
    mixed = mixed[:, :wide] + mixed[:, wide:]
    re, im = mixed[:LANES], mixed[LANES:]
    tc, ts = twist_ref[0], twist_ref[1]
    turned = jnp.concatenate([re * tc + im * ts, im * tc - re * ts], axis=1)
    high, low = split(turned)
    pair = dot(jnp.concatenate([high, low], axis=0), two_ref[0])
    spec = pair[:LANES] + pair[LANES:] + dot(high, two_ref[1])

    lane = lax.broadcasted_iota(jnp.int32, (16, 2 * half), 1)
    low64 = lax.broadcasted_iota(jnp.int32, (64, 2 * half), 1) < half
    low16 = lane < half
    sides = []
    square = jnp.zeros((LANES, 2 * half), jnp.float32)
    for part_index in range(2):
        o = spec[:, part_index * 2 * half:(part_index + 1) * 2 * half]
        square = square + o * o
        before = jnp.where(lane == 0, 0.0, pltpu.roll(o[LANES - 16:], 1, 1))
        after = jnp.where(lane == 2 * half - 1, 0.0, pltpu.roll(o[:16], 2 * half - 1, 1))
        sides.append(
            jnp.concatenate(
                [
                    jnp.where(low16, before, o[48:64]),
                    jnp.where(low64, o[:64], o[64:]),
                    jnp.where(low16, o[64:80], after),
                    jnp.zeros((32, 2 * half), jnp.float32),
                ],
                axis=0,
            ).astype(jnp.bfloat16)
        )
    energy_ref[0] = jnp.sum(square) * 0.5
    sr, si = sides
    window = jnp.concatenate(
        [jnp.concatenate([sr, si], axis=1), jnp.concatenate([-si, sr], axis=1)], axis=0
    )
    best = jnp.zeros((accels, 2 * half), jnp.float32)
    group = 8
    for g in range(LANES // 2 // group):
        out = dot(tmat[g * group * accels:(g + 1) * group * accels, :], window)
        for kk in range(group):
            rr = out[kk * accels:(kk + 1) * accels, :2 * half]
            ii = out[kk * accels:(kk + 1) * accels, 2 * half:]
            best = jnp.maximum(best, rr * rr + ii * ii)
    best = jnp.maximum(best, pltpu.roll(best, half, 1))
    peaks_ref[0] = best[:, :half]
    everything(early, early_out_sem).wait()
    everything(late, late_out_sem).wait()


def finish(found_ref, total_ref, peaks_ref, energy_ref):
    peaks_ref[...] = found_ref[...]
    energy_ref[0] = total_ref[0]


def solution(mesh):
    fft, chan = mesh.shape["fft"], mesh.shape["chan"]
    cores = 2
    xs = chan // cores

    def body(filterbank, delays, template_bank, accel_index):
        channels, samples = filterbank.shape
        dms = delays.shape[1]
        accels = accel_index.shape[0]
        length = samples * fft
        blocks = samples // LANES
        wide = length // LANES
        cut = blocks // 2 + MAXD
        rest = blocks + MAXD - cut
        one, twist, two = tables(length, channels * chan)
        bank = template_bank.transpose(0, 2, 1)
        accel = accel_index[None, :]
        f32, bf16 = jnp.float32, jnp.bfloat16
        dma = pltpu.SemaphoreType.DMA
        hbm = pl.BlockSpec(memory_space=pltpu.HBM)
        vmem = pl.BlockSpec(memory_space=pltpu.VMEM)

        def like(a):
            return pltpu.VMEM(a.shape, a.dtype)

        found, total = pl.pallas_call(
            functools.partial(kernel, (fft, xs, cores, dms, blocks)),
            out_shape=(
                pltpu.VMEM((1, accels, wide // 2), f32),
                pltpu.SMEM((1,), f32),
            ),
            in_specs=[hbm] * 7,
            out_specs=(vmem, pl.BlockSpec(memory_space=pltpu.SMEM)),
            scratch_shapes=[
                pltpu.VMEM((dms, channels), jnp.int32),
                pltpu.VMEM((channels, samples), bf16),
                pltpu.VMEM((MAXD * dms, channels), bf16),
                pltpu.VMEM((PARTS, (blocks + MAXD) * dms // PARTS, LANES), f32),
                pltpu.VMEM((dms, rest, LANES), bf16),
                pltpu.VMEM((dms, cut, LANES), bf16),
                pltpu.VMEM((dms, rest, LANES), bf16),
                pltpu.VMEM((dms, cut, LANES), bf16),
                pltpu.VMEM((wide, LANES), f32),
                like(bank), like(accel), like(one), like(twist), like(two),
                pltpu.VMEM((LANES // 2 * accels, 2 * LANES), bf16),
                dma, dma((len(SEGMENTS),)), dma((5,)), dma, dma, dma, dma,
            ],
            compiler_params=pltpu.CompilerParams(
                collective_id=0, has_side_effects=True, vmem_limit_bytes=56 * 2 ** 20
            ),
            name="search",
        )(filterbank, delays.T, bank, accel, one, twist, two)

        return pl.pallas_call(
            finish,
            out_shape=(
                jax.ShapeDtypeStruct(found.shape, f32),
                jax.ShapeDtypeStruct(total.shape, f32),
            ),
            in_specs=[vmem, pl.BlockSpec(memory_space=pltpu.SMEM)],
            out_specs=(vmem, pl.BlockSpec(memory_space=pltpu.SMEM)),
            name="finish",
        )(pltpu.with_memory_space_constraint(found, pltpu.VMEM), pltpu.with_memory_space_constraint(total, pltpu.SMEM))

    in_specs = (P(("beam", "chan"), "fft"), P("chan", None), P(), P())
    out_specs = (P(("beam", "fft", "chan"), None, None), P(("beam", "fft", "chan")))
    return jax.shard_map(body, mesh=mesh, in_specs=in_specs, out_specs=out_specs, check_vma=False)
```
